256 devices in a mesh: design: 8 (over x, core), pts: 32 (over z, y).
Axes of the slice: x: 4, y: 4, z: 8, core: 2. Of those that a mesh axis runs over, the one named last changes fastest.
Arguments:
- points: bfloat16 [65536, 256], P(('design', 'pts')), parts along dimension 0, may hold values from -6 to 6
- geometry: bfloat16 [131072, 256], P(('design', 'pts')), parts along dimension 0, may hold values from -6 to 6
- counts: int32 [256], P(('design', 'pts')), parts along dimension 0, may hold values from 128 to 256, as said below
- cotangent: bfloat16 [65536, 256], P(('design', 'pts')), parts along dimension 0, may hold values from -0.0625 to 0.0625
- gain_attn: float32 [256], replicated, may hold values from 0.5 to 1.5
- w_feat: bfloat16 [256, 256], replicated, may hold values from -0.375 to 0.375
- w_mid: bfloat16 [256, 256], replicated, may hold values from -0.375 to 0.375
- w_slice: bfloat16 [32, 256], replicated, may hold values from -1 to 1
- sharpness: float32 [8], replicated, may hold values from 0.5 to 6
- w_query: float32 [32, 32], replicated, may hold values from -0.5 to 0.5
- w_key: float32 [32, 32], replicated, may hold values from -0.5 to 0.5
- w_value: float32 [32, 32], replicated, may hold values from -1 to 1
- w_out: bfloat16 [256, 256], replicated, may hold values from -0.375 to 0.375
- gain_mlp: float32 [256], replicated, may hold values from 0.5 to 1.5
- w_up: bfloat16 [256, 1024], replicated, may hold values from -0.375 to 0.375
- w_down: bfloat16 [1024, 256], replicated, may hold values from -0.1875 to 0.1875
Outputs:
- layer_out: bfloat16 [65536, 256], P(('design', 'pts')), parts along dimension 0
- grad_feat: float32 [2048, 256], P(('design', 'pts')), parts along dimension 0
- grad_mid: float32 [2048, 256], P(('design', 'pts')), parts along dimension 0
- grad_out: float32 [2048, 256], P(('design', 'pts')), parts along dimension 0
- grad_up: float32 [2048, 1024], P(('design', 'pts')), parts along dimension 0
- grad_down: float32 [8192, 256], P(('design', 'pts')), parts along dimension 0
- grad_slice: float32 [256, 256], P('design'), parts along dimension 0
- grad_mix: float32 [24, 32, 32], P('design'), parts along dimension 0
The draws below stay inside these ranges and needn't reach their ends.
There are 8 independent parts, one for each index of `design`. The reference program is written for one: setup_inputs(seed, part) draws one part's arguments, and reference() takes and returns one part's arrays. A program takes and returns all parts, laid end to end along the dimension named above; an argument that names none is the same for every part. Nothing has to cross between parts.
Inputs may be any that keep to these rules, and one draw needn't show every extreme that they name: `counts`: every device of a design holds at least half of its 256 slots live, and some device holds all of them.
All inputs are finite; a program needn't handle non-finite values.
Results may differ from the reference program's by a relative error of at most 0.017.
The reference program's roundings to bfloat16 on the way (of `mixed_low`, `attended`, `second_low`, `hidden`, `grad_upper`, `grad_resid` and `grad_att`) count: a program that leaves them out, or rounds other values in their place, can miss the bound.
Values sent between devices are 32-bit elements; how exact they have to be, the bound alone decides.
A program may use at most 64 MiB of HBM per device.

```python
import math
import jax
import jax.numpy as jnp
from jax import lax

D = 256
HEADS = 8
DH = 32
SLICES = 256
FF = 1024
P_DEV = 256
POINTS = 8192
GEO_POINTS = 16384
N_PTS = 32


def draw_counts(key, part):
    level_key = jax.random.fold_in(key, 11)
    pick_key = jax.random.fold_in(key, 12)
    levels = jax.random.randint(level_key, (N_PTS,), P_DEV // 2, P_DEV + 1)
    chosen = jax.random.randint(pick_key, (), 0, N_PTS)
    return jnp.where(jnp.arange(N_PTS) == chosen, P_DEV, levels).astype(jnp.int32)


def draw_sharpness(key, part):
    base = jax.random.uniform(jax.random.fold_in(key, 21), (HEADS,), jnp.float32, math.log(0.5), math.log(4.0))
    return jnp.exp(base).astype(jnp.float32)


def draw_points(key, part):
    noise_key = jax.random.fold_in(key, 31)
    scale_key = jax.random.fold_in(key, 32)
    noise = jnp.clip(jax.random.normal(noise_key, (POINTS, D), jnp.float32), -6.0, 6.0)
    scales = jnp.exp(jax.random.uniform(scale_key, (POINTS, 1), jnp.float32, math.log(1.0 / 32.0), math.log(1.0 / 12.0)))
    return (noise * scales).astype(jnp.bfloat16)


def block_levels(rng, dims, cuts, least, top_value):
    def one(axis_at, shards_of):
        steps = jax.random.uniform(jax.random.fold_in(jax.random.fold_in(rng, 6), axis_at), (shards_of,), jnp.float32, least / len(cuts), top_value / len(cuts))
        return jnp.repeat(jnp.exp(steps), dims[axis_at] // shards_of).reshape((-1,) + (1,) * (len(dims) - axis_at - 1))

    level = one(*cuts[0])
    for cut in cuts[1:]:
        level = level * one(*cut)
    return level


def normal_values(key, extent, scale, limit, cuts=(), kind=jnp.bfloat16):
    result = scale * jax.random.normal(key, extent, jnp.float32)
    if cuts:
        result = result * block_levels(key, extent, cuts, -0.22, 0.18)
    return jnp.clip(result, -limit, limit).astype(kind)


def setup_inputs(seed: int = 0, part: int = 0) -> dict:
    key_list = jax.random.split(jax.random.key(seed), 17)
    part_keys = jax.random.split(jax.random.fold_in(key_list[16], part), 17)
    points = draw_points(jax.random.fold_in(jax.random.fold_in(key_list[16], part), 71), part)
    geometry = normal_values(part_keys[1], (GEO_POINTS, D), 1.0, 6.0, ((0, 32),))
    counts = draw_counts(jax.random.fold_in(jax.random.fold_in(key_list[16], part), 71), part)
    cotangent = normal_values(part_keys[3], (POINTS, D), ((P_DEV * N_PTS) ** -0.5), 0.0625, ((0, 32),))
    gain_attn = jnp.clip(1.0 + 0.1 * jax.random.normal(key_list[4], (D,), jnp.float32), 0.5, 1.5)
    w_feat = normal_values(key_list[5], (D, D), D ** -0.5, 0.375)
    w_mid = normal_values(key_list[6], (D, D), D ** -0.5, 0.375)
    w_slice = normal_values(key_list[7], (DH, SLICES), DH ** -0.5, 1.0)
    sharpness = draw_sharpness(jax.random.fold_in(key_list[16], 71), part)
    w_query = normal_values(key_list[9], (DH, DH), (DH * 4) ** -0.5, 0.5, (), jnp.float32)
    w_key = normal_values(key_list[10], (DH, DH), (DH * 4) ** -0.5, 0.5, (), jnp.float32)
    w_value = normal_values(key_list[11], (DH, DH), DH ** -0.5, 1.0, (), jnp.float32)
    w_out = normal_values(key_list[12], (D, D), D ** -0.5, 0.375)
    gain_mlp = jnp.clip(1.0 + 0.1 * jax.random.normal(key_list[13], (D,), jnp.float32), 0.5, 1.5)
    w_up = normal_values(key_list[14], (D, FF), D ** -0.5, 0.375)
    w_down = normal_values(key_list[15], (FF, D), FF ** -0.5, 0.1875)
    return dict(points=points, geometry=geometry, counts=counts, cotangent=cotangent, gain_attn=gain_attn, w_feat=w_feat, w_mid=w_mid, w_slice=w_slice, sharpness=sharpness, w_query=w_query, w_key=w_key, w_value=w_value, w_out=w_out, gain_mlp=gain_mlp, w_up=w_up, w_down=w_down)


def layer_norm(inputs, gain):
    inputs = inputs.astype(jnp.float32)
    centre = lax.optimization_barrier(jnp.mean(inputs, axis=-1, keepdims=True))
    shifted = inputs - centre
    spread = lax.optimization_barrier(jnp.mean(shifted * shifted, axis=-1, keepdims=True))
    return shifted * lax.rsqrt(spread + 1e-05) * gain

def gelu_tanh(inputs):
    return jax.nn.gelu(inputs, approximate=True)

def project(inputs, gain_attn, w_feat, w_mid):
    normed = layer_norm(inputs, gain_attn).astype(jnp.bfloat16)
    features = jnp.dot(normed, w_feat, preferred_element_type=jnp.float32).astype(jnp.bfloat16)
    middle = jnp.dot(normed, w_mid, preferred_element_type=jnp.float32).astype(jnp.bfloat16)
    return (normed, features, middle)

def slice_shares(middle, w_slice, sharpness):
    count = middle.shape[0]
    heads = sharpness.shape[0]
    logits = jnp.dot(middle.reshape(count * heads, -1), w_slice, preferred_element_type=jnp.float32)
    logits = logits.reshape(count, heads, -1) * sharpness[None, :, None]
    largest = lax.optimization_barrier(jnp.max(logits, axis=-1, keepdims=True))
    powers = jnp.exp(logits - largest)
    return powers / lax.optimization_barrier(jnp.sum(powers, axis=-1, keepdims=True))

def mix_tokens(numerator, denominator, geo_numerator, geo_denominator, w_query, w_key, w_value):
    highest = lax.Precision.HIGHEST
    field_tokens = numerator / (denominator + 1e-05)[:, :, None]
    geo_tokens = geo_numerator / (geo_denominator + 1e-05)[:, :, None]
    both = jnp.concatenate([field_tokens, geo_tokens], axis=1)
    query = jnp.einsum('hme,ef->hmf', field_tokens, w_query, precision=highest)
    key_rows = jnp.einsum('hke,ef->hkf', both, w_key, precision=highest)
    value_rows = jnp.einsum('hke,ef->hkf', both, w_value, precision=highest)
    scores = jnp.einsum('hmf,hkf->hmk', query, key_rows, precision=highest) / math.sqrt(w_query.shape[0])
    largest = lax.optimization_barrier(jnp.max(scores, axis=-1, keepdims=True))
    powers = jnp.exp(scores - largest)
    attention = powers / lax.optimization_barrier(jnp.sum(powers, axis=-1, keepdims=True))
    return jnp.einsum('hmk,hkf->hmf', attention, value_rows, precision=highest)

def mlp_pass(inputs, seed_block, weights_low, mixed_low, w_out, gain_mlp, w_up, w_down):
    count, heads, slices = weights_low.shape
    attended = jnp.einsum('bhm,hme->bhe', weights_low.astype(jnp.float32), mixed_low.astype(jnp.float32))
    attended = attended.reshape(count, -1).astype(jnp.bfloat16)
    residual = inputs.astype(jnp.float32) + jnp.dot(attended, w_out, preferred_element_type=jnp.float32)

    def mlp_norm(values_in):
        return layer_norm(values_in, gain_mlp)
    second, norm_back = jax.vjp(mlp_norm, residual)
    second_low = second.astype(jnp.bfloat16)
    upper = jnp.dot(second_low, w_up, preferred_element_type=jnp.float32)
    active, gelu_back = jax.vjp(gelu_tanh, upper)
    hidden = active.astype(jnp.bfloat16)
    layer_block = (residual + jnp.dot(hidden, w_down, preferred_element_type=jnp.float32)).astype(jnp.bfloat16)
    grad_hidden = jnp.dot(seed_block, w_down.T, preferred_element_type=jnp.float32)
    grad_upper = gelu_back(grad_hidden)[0].astype(jnp.bfloat16)
    grad_second = jnp.dot(grad_upper, w_up.T, preferred_element_type=jnp.float32)
    grad_resid = (seed_block.astype(jnp.float32) + norm_back(grad_second)[0]).astype(jnp.bfloat16)
    grad_att = jnp.dot(grad_resid, w_out.T, preferred_element_type=jnp.float32).astype(jnp.bfloat16)
    return (layer_block, attended, second_low, hidden, grad_upper, grad_resid, grad_att)

def point_back(shares, valid, weights_low, features, grad_att, mixed_low, numer_low, denom_grad, sharpness):
    count, heads, slices = shares.shape
    feats = features.reshape(count, heads, -1).astype(jnp.float32)
    grad_weights = jnp.einsum('bhe,hme->bhm', feats, numer_low.astype(jnp.float32)) + denom_grad[None]
    if grad_att is not None:
        grad_weights = grad_weights + jnp.einsum('bhe,hme->bhm', grad_att.reshape(count, heads, -1).astype(jnp.float32), mixed_low.astype(jnp.float32))
    grad_weights = grad_weights * valid[:, None, None]
    inner = lax.optimization_barrier(jnp.sum(shares * grad_weights, axis=-1, keepdims=True))
    logit_low = (shares * (grad_weights - inner) * sharpness[None, :, None]).astype(jnp.bfloat16)
    grad_features = jnp.einsum('bhm,hme->bhe', weights_low.astype(jnp.float32), numer_low.astype(jnp.float32))
    grad_features = grad_features.reshape(count, -1).astype(jnp.bfloat16)
    return (logit_low, grad_features)

def middle_back(logit_low, middle, w_slice):
    count, heads, slices = logit_low.shape
    flat = logit_low.reshape(count * heads, slices)
    grad_middle = jnp.dot(flat, w_slice.T, preferred_element_type=jnp.float32).reshape(count, -1).astype(jnp.bfloat16)
    slice_term = jnp.dot(middle.reshape(count * heads, -1).T, flat, preferred_element_type=jnp.float32)
    return (grad_middle, slice_term)

def reference(points, geometry, counts, cotangent, gain_attn, w_feat, w_mid, w_slice, sharpness, w_query, w_key, w_value, w_out, gain_mlp, w_up, w_down):
    total = points.shape[0]
    index = jnp.arange(total, dtype=jnp.int32)
    valid = (index % P_DEV < counts[index // P_DEV]).astype(jnp.float32)
    geo_valid = jnp.ones((geometry.shape[0],), jnp.float32)

    def forward_sums(inputs, keep):
        block = math.gcd(inputs.shape[0], 512)

        def step(carry, pieces):
            rows_in, keep_block = pieces
            normed, features, middle = project(rows_in, gain_attn, w_feat, w_mid)
            shares = slice_shares(middle, w_slice, sharpness)
            weights = shares * keep_block[:, None, None]
            weights_low = weights.astype(jnp.bfloat16)
            numerator = jnp.einsum('bhm,bhe->hme', weights_low.astype(jnp.float32), features.reshape(block, HEADS, DH).astype(jnp.float32))
            return ((carry[0] + numerator, carry[1] + lax.optimization_barrier(jnp.sum(weights, axis=0))), None)
        start = (jnp.zeros((HEADS, SLICES, DH), jnp.float32), jnp.zeros((HEADS, SLICES), jnp.float32))
        sums, _ = lax.scan(step, start, (inputs.reshape(-1, block, D), keep.reshape(-1, block)))
        return sums
    field_sums = forward_sums(points, valid)
    geo_sums = forward_sums(geometry, geo_valid)
    mixed, token_back = jax.vjp(mix_tokens, field_sums[0], field_sums[1], geo_sums[0], geo_sums[1], w_query, w_key, w_value)
    mixed_low = mixed.astype(jnp.bfloat16)
    block = math.gcd(total, 512)

    def mlp_step(carry, pieces):
        rows_in, keep_block, seed_block = pieces
        normed, features, middle = project(rows_in, gain_attn, w_feat, w_mid)
        shares = slice_shares(middle, w_slice, sharpness)
        weights_low = (shares * keep_block[:, None, None]).astype(jnp.bfloat16)
        layer_block, attended, second_low, hidden, grad_upper, grad_resid, grad_att = mlp_pass(rows_in, seed_block, weights_low, mixed_low, w_out, gain_mlp, w_up, w_down)
        down_acc, up_acc, out_acc, mixed_acc = carry
        down_acc = down_acc + jnp.dot(hidden.T, seed_block, preferred_element_type=jnp.float32)
        up_acc = up_acc + jnp.dot(second_low.T, grad_upper, preferred_element_type=jnp.float32)
        out_acc = out_acc + jnp.dot(attended.T, grad_resid, preferred_element_type=jnp.float32)
        mixed_acc = mixed_acc + jnp.einsum('bhm,bhe->hme', weights_low.astype(jnp.float32), grad_att.reshape(block, HEADS, DH).astype(jnp.float32))
        return ((down_acc, up_acc, out_acc, mixed_acc), (layer_block, grad_att))
    start = (jnp.zeros((FF, D), jnp.float32), jnp.zeros((D, FF), jnp.float32), jnp.zeros((D, D), jnp.float32), jnp.zeros((HEADS, SLICES, DH), jnp.float32))
    accum, outputs = lax.scan(mlp_step, start, (points.reshape(-1, block, D), valid.reshape(-1, block), cotangent.reshape(-1, block, D)))
    grad_down, grad_up, grad_out, mixed_grad = accum
    layer_out = outputs[0].reshape(total, D)
    grad_att_all = outputs[1]
    grads = token_back(mixed_grad)
    numer_low = grads[0].astype(jnp.bfloat16)
    geo_numer_low = grads[2].astype(jnp.bfloat16)
    grad_mix = jnp.stack([grads[4], grads[5], grads[6]])

    def back_sums(inputs, keep, att_blocks, numer_use, denom_use):
        size = math.gcd(inputs.shape[0], 512)

        def step(carry, pieces):
            rows_in, keep_block, att_block = pieces
            normed, features, middle = project(rows_in, gain_attn, w_feat, w_mid)
            shares = slice_shares(middle, w_slice, sharpness)
            weights_low = (shares * keep_block[:, None, None]).astype(jnp.bfloat16)
            logit_low, grad_features = point_back(shares, keep_block, weights_low, features, att_block, mixed_low, numer_use, denom_use, sharpness)
            grad_middle, slice_term = middle_back(logit_low, middle, w_slice)
            feat_acc, mid_acc, slice_acc = carry
            feat_acc = feat_acc + jnp.dot(normed.T, grad_features, preferred_element_type=jnp.float32)
            mid_acc = mid_acc + jnp.dot(normed.T, grad_middle, preferred_element_type=jnp.float32)
            return ((feat_acc, mid_acc, slice_acc + slice_term), None)
        if att_blocks is None:

            def plain_step(carry, pieces):
                return step(carry, (pieces[0], pieces[1], None))
            scan_fn = plain_step
            scanned = (inputs.reshape(-1, size, D), keep.reshape(-1, size))
        else:
            scan_fn = step
            scanned = (inputs.reshape(-1, size, D), keep.reshape(-1, size), att_blocks)
        init = (jnp.zeros((D, D), jnp.float32), jnp.zeros((D, D), jnp.float32), jnp.zeros((DH, SLICES), jnp.float32))
        sums, _ = lax.scan(scan_fn, init, scanned)
        return sums
    field_back = back_sums(points, valid, grad_att_all, numer_low, grads[1])
    geo_back = back_sums(geometry, geo_valid, None, geo_numer_low, grads[3])
    grad_feat = field_back[0] + geo_back[0]
    grad_mid = field_back[1] + geo_back[1]
    grad_slice = field_back[2] + geo_back[2]
    return (layer_out, grad_feat, grad_mid, grad_out, grad_up, grad_down, grad_slice, grad_mix)
```

```python
import functools
import math

import jax
import jax.numpy as jnp
from jax import lax
from jax.experimental import pallas as pl
from jax.experimental.pallas import tpu as pltpu
from jax.sharding import PartitionSpec as P

F32 = jnp.float32
BF16 = jnp.bfloat16
HIGH = lax.Precision.HIGHEST
NY = 4
NZ = 8
HEADS = 8
DH = 32
M = 256
D = 256
FF = 1024
RB = 256
SUMS = 72
BIG = 72
SMALL = 16
EPS = 1e-05
VMEM_BYTES = 64000000
ORDER = (4, 3, 5, 2, 6, 1, 7)


def nn(a, b, precision=None):
    return lax.dot_general(
        a, b, (((1,), (0,)), ((), ())), precision=precision, preferred_element_type=F32
    )


def nt(a, b, precision=None):
    return lax.dot_general(
        a, b, (((1,), (1,)), ((), ())), precision=precision, preferred_element_type=F32
    )


def tn(a, b, precision=None):
    return lax.dot_general(
        a, b, (((0,), (0,)), ((), ())), precision=precision, preferred_element_type=F32
    )


def norm_parts(x):
    centre = jnp.mean(x, axis=-1, keepdims=True)
    shifted = x - centre
    spread = jnp.mean(shifted * shifted, axis=-1, keepdims=True)
    scale = lax.rsqrt(spread + EPS)
    return shifted * scale, scale


def place():
    me = lax.axis_index("pts")
    return lax.div(me, NY), lax.rem(me, NY)


def peer_z(z, y, k):
    return {"pts": lax.rem(z + k, NZ) * NY + y}


def peer_y(z, y, k):
    return {"pts": z * NY + lax.rem(y + k, NY)}


def greet(z, y):
    barrier = pltpu.get_barrier_semaphore()
    for k in range(1, NZ):
        pl.semaphore_signal(barrier, inc=1, device_id=peer_z(z, y, k), device_id_type=pl.DeviceIdType.MESH)
    for k in range(1, NY):
        pl.semaphore_signal(barrier, inc=1, device_id=peer_y(z, y, k), device_id_type=pl.DeviceIdType.MESH)


def meet():
    pl.semaphore_wait(pltpu.get_barrier_semaphore(), NZ - 1 + NY - 1)


def send(src, dst, sems, slot, device):
    return pltpu.make_async_remote_copy(
        src_ref=src,
        dst_ref=dst,
        send_sem=sems.at[0, slot],
        recv_sem=sems.at[1, slot],
        device_id=device,
        device_id_type=pl.DeviceIdType.MESH,
    )


def first_kernel(
    points,
    geometry,
    counts,
    gain,
    w_feat,
    w_mid,
    w_slice,
    sharp,
    w_query,
    w_key,
    w_value,
    normed_out,
    feat_out,
    mid_out,
    shares_out,
    wlow_out,
    wsm_out,
    mixed_out,
    attn_out,
    both_out,
    query_out,
    keyval_out,
    sums_out,
    part,
    zbuf,
    ybuf,
    mbuf,
    feat_t,
    sem_z,
    sem_y,
    sem_m,
):
    z, y = place()
    greet(z, y)
    wsm_out[...] = jnp.zeros_like(wsm_out)
    for h in range(HEADS):
        wsm_out[h, h * DH : (h + 1) * DH, :] = w_slice[...]
    for b in range(3):
        rows = slice(b * RB, (b + 1) * RB)
        x = points[...] if b == 0 else geometry[(b - 1) * RB : b * RB, :]
        normed = (norm_parts(x.astype(F32))[0] * gain[...]).astype(BF16)
        normed_out[rows, :] = normed
        feats = nn(normed, w_feat[...])
        feat_out[rows, :] = feats.astype(BF16)
        feat_t[:, rows] = feats.T.astype(BF16)
        mid_out[rows, :] = nn(normed, w_mid[...]).astype(BF16)
    live = lax.broadcasted_iota(jnp.int32, (RB, 1), 0) < counts[0]
    valid = jnp.where(live, 1.0, 0.0).astype(F32)
    meet()

    def head_step(k, carry):
        h = lax.rem(z + 1 + k, NZ)
        weight = wsm_out[h]
        factor = sharp[h]
        row = pl.multiple_of(h * DH, DH)
        numers = []
        denoms = []
        for b in range(3):
            rows = slice(b * RB, (b + 1) * RB)
            logits = nn(mid_out[rows, :], weight) * factor
            powers = jnp.exp(logits - jnp.max(logits, axis=-1, keepdims=True))
            shares = powers * (1.0 / jnp.sum(powers, axis=-1, keepdims=True))
            shares_out[h, rows, :] = shares
            weights = shares * valid if b == 0 else shares
            low = weights.astype(BF16)
            wlow_out[h, rows, :] = low
            denoms.append(jnp.sum(weights, axis=0, keepdims=True))
            numers.append(nn(feat_t[pl.ds(row, DH), rows], low))
        part[h, 0:DH, :] = numers[0]
        part[h, DH : 2 * DH, :] = numers[1] + numers[2]
        pick = lax.broadcasted_iota(jnp.int32, (8, M), 0)
        part[h, 2 * DH : SUMS, :] = jnp.where(
            pick == 0, denoms[0], jnp.where(pick == 1, denoms[1] + denoms[2], 0.0)
        )

        @pl.when(k < NZ - 1)
        def _():
            send(part.at[h], zbuf.at[k], sem_z, k, peer_z(z, y, k + 1)).start()

        return carry

    lax.fori_loop(0, NZ, head_step, 0)
    total = part[z]
    for k in range(NZ - 1):
        send(part.at[0], zbuf.at[k], sem_z, k, peer_z(z, y, k + 1)).wait_recv()
        total = total + zbuf[k]
    ybuf[0] = total
    copies = [send(ybuf.at[0], ybuf.at[k], sem_y, k - 1, peer_y(z, y, k)) for k in range(1, NY)]
    for copy in copies:
        copy.start()
    for copy in copies:
        copy.wait_recv()
    sums = ybuf[y]
    for other in range(1, NY):
        sums = sums + ybuf[lax.rem(y + NY - other, NY)]
    sums_out[...] = sums
    field = sums[0:DH] / (sums[2 * DH : 2 * DH + 1] + EPS)
    geo = sums[DH : 2 * DH] / (sums[2 * DH + 1 : 2 * DH + 2] + EPS)
    both_out[:, 0:M] = field
    both_out[:, M : 2 * M] = geo
    both = both_out[...]
    query = tn(w_query[...], field, HIGH)
    keys = tn(w_key[...], both, HIGH)
    values = tn(w_value[...], both, HIGH)
    query_out[...] = query
    keyval_out[0] = keys
    keyval_out[1] = values
    scores = tn(keys, query, HIGH) * (1.0 / math.sqrt(DH))
    powers = jnp.exp(scores - jnp.max(scores, axis=0, keepdims=True))
    attention = powers * (1.0 / jnp.sum(powers, axis=0, keepdims=True))
    attn_out[...] = attention
    mbuf[z] = nn(values, attention, HIGH)
    copies = [
        send(mbuf.at[z], mbuf.at[z], sem_m, k - 1, peer_z(z, y, k)) for k in ORDER
    ]
    for copy in copies:
        copy.start()
    for copy in copies:
        copy.wait_recv()
    mixed_out[...] = mbuf[...]
    for copy in copies:
        copy.wait_send()
    for k in range(1, NY):
        send(ybuf.at[0], ybuf.at[k], sem_y, k - 1, peer_y(z, y, k)).wait_send()
    for k in range(NZ - 1):
        send(part.at[0], zbuf.at[k], sem_z, k, peer_z(z, y, k + 1)).wait_send()


def second_kernel(
    points,
    cotangent,
    counts,
    wlow,
    shares,
    normed,
    feats,
    mids,
    wsm,
    mixed,
    attn,
    both_in,
    query_in,
    keyval,
    sums_in,
    sharp,
    gain,
    w_out,
    w_up,
    w_down,
    w_query,
    w_key,
    w_value,
    layer_out,
    feat_grad,
    mid_grad,
    out_grad,
    up_grad,
    down_grad,
    slice_grad,
    mix_grad,
    mixm,
    num_m,
    geo_m,
    low_up,
    low_hidden,
    grad_up_low,
    norm_hat,
    att_rows,
    res_rows,
    att_grad,
    mid_t,
    normed_t,
    acc_feat,
    acc_mid,
    mg_part,
    mg_z,
    mg_y,
    gbuf,
    mix_buf,
    big,
    big_y,
    big_stage,
    big_z,
    small,
    small_y,
    small_stage,
    small_z,
    slice_part,
    slice_y,
    slice_z,
    slice_all,
    sem_mz,
    sem_my,
    sem_g,
    sem_mix,
    sem_by,
    sem_bz,
    sem_sy,
    sem_sz,
    sem_ly,
    sem_lz,
    sem_la,
):
    z, y = place()
    greet(z, y)
    mixm[...] = jnp.zeros_like(mixm)
    for h in range(HEADS):
        mixm[h, h * DH : (h + 1) * DH, :] = mixed[h].astype(BF16)
    attended = nt(wlow[0, 0:RB, :], mixm[0])
    for h in range(1, HEADS):
        attended = attended + nt(wlow[h, 0:RB, :], mixm[h])
    attended = attended.astype(BF16)
    att_rows[...] = attended
    residual = points[...].astype(F32) + nn(attended, w_out[...])
    hat, scale = norm_parts(residual)
    second_low = (hat * gain[...]).astype(BF16)
    low_up[...] = second_low
    norm_hat[...] = hat
    seed = cotangent[...]
    const = math.sqrt(2.0 / math.pi)
    layer = residual
    grad_second = jnp.zeros((RB, D), F32)
    for j in range(FF // D):
        cols = slice(j * D, (j + 1) * D)
        upper = nn(second_low, w_up[:, cols])
        square = upper * upper
        tanh = jnp.tanh(const * upper * (1.0 + 0.044715 * square))
        half = 0.5 * (1.0 + tanh)
        hidden = (upper * half).astype(BF16)
        low_hidden[:, cols] = hidden
        layer = layer + nn(hidden, w_down[cols, :])
        slope = half + 0.5 * upper * (1.0 - tanh * tanh) * (const * (1.0 + 3.0 * 0.044715 * square))
        grad_upper = (nt(seed, w_down[cols, :]) * slope).astype(BF16)
        grad_up_low[:, cols] = grad_upper
        grad_second = grad_second + nt(grad_upper, w_up[:, cols])
    layer_out[...] = layer.astype(BF16)
    hat = norm_hat[...]
    scaled = grad_second * gain[...]
    back = scale * (
        scaled
        - jnp.mean(scaled, axis=-1, keepdims=True)
        - hat * jnp.mean(scaled * hat, axis=-1, keepdims=True)
    )
    grad_resid = (seed.astype(F32) + back).astype(BF16)
    res_rows[...] = grad_resid
    grad_att = nt(grad_resid, w_out[...])
    att_grad[...] = grad_att.astype(BF16)
    att_t = grad_att.T.astype(BF16)
    for h in range(HEADS):
        mg_part[h] = nn(att_t[h * DH : (h + 1) * DH, :], wlow[h, 0:RB, :])
    meet()
    mz_copies = [
        send(mg_part.at[lax.rem(z + k, NZ)], mg_z.at[k - 1], sem_mz, k - 1, peer_z(z, y, k))
        for k in ORDER
    ]
    for copy in mz_copies:
        copy.start()
    seed = cotangent[...]
    for j in range(FF // D):
        cols = slice(j * D, (j + 1) * D)
        down = nn(low_hidden[:, cols].astype(F32).T.astype(BF16), seed)
        big[2 * j : 2 * j + 2, :, 0:DH, :] = down.reshape(2, NY, DH, D)
        up = nn(low_up[...].astype(F32).T.astype(BF16), grad_up_low[:, cols])
        big[:, :, DH + 8 * j : DH + 8 * j + 8, :] = up.reshape(NZ, NY, 8, D)
    out = nn(att_rows[...].astype(F32).T.astype(BF16), res_rows[...])
    big[:, :, 2 * DH : BIG, :] = out.reshape(NZ, NY, 8, D)
    num_m[...] = jnp.zeros_like(num_m)
    geo_m[...] = jnp.zeros_like(geo_m)
    for copy in mz_copies:
        copy.wait_recv()
    total = mg_part[z]
    for k in range(NZ - 1):
        total = total + mg_z[k]
    mg_y[0] = total
    my_copies = [send(mg_y.at[0], mg_y.at[k], sem_my, k - 1, peer_y(z, y, k)) for k in range(1, NY)]
    for copy in my_copies:
        copy.start()
    by_copies = [
        send(big.at[:, lax.rem(y + k, NY)], big_y.at[k - 1], sem_by, k - 1, peer_y(z, y, k))
        for k in (2, 1, 3)
    ]
    for copy in by_copies:
        copy.start()
    for b in range(3):
        rows = slice(b * RB, (b + 1) * RB)
        mid_t[:, rows] = mids[rows, :].astype(F32).T.astype(BF16)
        normed_t[:, rows] = normed[rows, :].astype(F32).T.astype(BF16)
    acc_feat[...] = jnp.zeros_like(acc_feat)
    acc_mid[...] = jnp.zeros_like(acc_mid)
    slice_part[...] = jnp.zeros_like(slice_part)
    for copy in my_copies:
        copy.wait_recv()
    grad = mg_y[y]
    for other in range(1, NY):
        grad = grad + mg_y[lax.rem(y + NY - other, NY)]
    attention = attn[...]
    keys = keyval[0]
    values = keyval[1]
    query = query_in[...]
    both = both_in[...]
    d_value = nt(grad, attention, HIGH)
    d_attn = tn(values, grad, HIGH)
    inner = jnp.sum(attention * d_attn, axis=0, keepdims=True)
    d_score = attention * (d_attn - inner) * (1.0 / math.sqrt(DH))
    d_query = nn(keys, d_score, HIGH)
    d_key = nt(query, d_score, HIGH)
    d_both = nn(w_key[...], d_key, HIGH) + nn(w_value[...], d_value, HIGH)
    d_field = d_both[:, 0:M] + nn(w_query[...], d_query, HIGH)
    d_geo = d_both[:, M : 2 * M]
    den = sums_in[2 * DH : 2 * DH + 1, :] + EPS
    geo_den = sums_in[2 * DH + 1 : 2 * DH + 2, :] + EPS
    scaled_field = d_field / den
    scaled_geo = d_geo / geo_den
    gbuf[z, 0:DH, :] = scaled_field
    gbuf[z, DH : 2 * DH, :] = scaled_geo
    den_grad = -jnp.sum(scaled_field * both[:, 0:M], axis=0, keepdims=True)
    geo_den_grad = -jnp.sum(scaled_geo * both[:, M : 2 * M], axis=0, keepdims=True)
    pick = lax.broadcasted_iota(jnp.int32, (8, M), 0)
    gbuf[z, 2 * DH : SUMS, :] = jnp.where(pick == 0, den_grad, jnp.where(pick == 1, geo_den_grad, 0.0))
    g_copies = [send(gbuf.at[z], gbuf.at[z], sem_g, k - 1, peer_z(z, y, k)) for k in range(1, NZ)]
    for copy in g_copies:
        copy.start()
    mix_buf[z, :, 0:DH] = nt(both[:, 0:M], d_query, HIGH)
    mix_buf[z, :, DH : 2 * DH] = nt(both, d_key, HIGH)
    mix_buf[z, :, 2 * DH : 3 * DH] = nt(both, d_value, HIGH)
    mix_buf[z, :, 3 * DH : 4 * DH] = jnp.zeros((DH, DH), F32)
    mix_copies = [
        send(mix_buf.at[z], mix_buf.at[z], sem_mix, k - 1, peer_z(z, y, k)) for k in ORDER
    ]
    for copy in mix_copies:
        copy.start()
    live = lax.broadcasted_iota(jnp.int32, (RB, 1), 0) < counts[0]
    valid = jnp.where(live, 1.0, 0.0).astype(F32)

    def head_step(k, carry):
        h = lax.rem(z + NZ - k, NZ)

        @pl.when(k > 0)
        def _():
            send(gbuf.at[z], gbuf.at[h], sem_g, k - 1, peer_z(z, y, k)).wait_recv()

        row = pl.multiple_of(h * DH, DH)
        num_m[h, pl.ds(row, DH), :] = gbuf[h, 0:DH, :].astype(BF16)
        geo_m[h, pl.ds(row, DH), :] = gbuf[h, DH : 2 * DH, :].astype(BF16)
        factor = sharp[h]
        for b in range(3):
            rows = slice(b * RB, (b + 1) * RB)
            token = num_m[h] if b == 0 else geo_m[h]
            grad_w = nn(feats[rows, :], token)
            if b == 0:
                grad_w = grad_w + nn(att_grad[...], mixm[h])
                grad_w = (grad_w + gbuf[h, 2 * DH : 2 * DH + 1, :]) * valid
            else:
                grad_w = grad_w + gbuf[h, 2 * DH + 1 : 2 * DH + 2, :]
            share = shares[h, rows, :]
            inside = jnp.sum(share * grad_w, axis=-1, keepdims=True)
            low = (share * (grad_w - inside) * factor).astype(BF16)
            slice_part[...] += nn(mid_t[pl.ds(row, DH), rows], low).reshape(NY, 8, M)
            acc_mid[rows, :] += nt(low, wsm[h])
            acc_feat[rows, :] += nt(wlow[h, rows, :], token)
        return carry

    lax.fori_loop(0, NZ, head_step, 0)
    feat_total = nn(normed_t[...], acc_feat[...].astype(BF16))
    mid_total = nn(normed_t[...], acc_mid[...].astype(BF16))
    small[:, :, 0:8, :] = feat_total.reshape(NZ, NY, 8, D)
    small[:, :, 8:16, :] = mid_total.reshape(NZ, NY, 8, D)
    sy_copies = [
        send(small.at[:, lax.rem(y + k, NY)], small_y.at[k - 1], sem_sy, k - 1, peer_y(z, y, k))
        for k in (2, 1, 3)
    ]
    ly_copies = [
        send(slice_part.at[lax.rem(y + k, NY)], slice_y.at[k - 1], sem_ly, k - 1, peer_y(z, y, k))
        for k in (2, 1, 3)
    ]
    for copy in sy_copies + ly_copies:
        copy.start()
    for copy in by_copies:
        copy.wait_recv()
    big_stage[...] = ((big[:, y] + big_y[0]) + big_y[1]) + big_y[2]
    bz_copies = [
        send(big_stage.at[lax.rem(z + k, NZ)], big_z.at[k - 1], sem_bz, k - 1, peer_z(z, y, k))
        for k in ORDER
    ]
    for copy in bz_copies:
        copy.start()
    for copy in sy_copies + ly_copies:
        copy.wait_recv()
    small_stage[...] = ((small[:, y] + small_y[0]) + small_y[1]) + small_y[2]
    slice_z[0] = ((slice_part[y] + slice_y[0]) + slice_y[1]) + slice_y[2]
    lz_copies = [send(slice_z.at[0], slice_z.at[k], sem_lz, k - 1, peer_z(z, y, k)) for k in ORDER]
    sz_copies = [
        send(small_stage.at[lax.rem(z + k, NZ)], small_z.at[k - 1], sem_sz, k - 1, peer_z(z, y, k))
        for k in ORDER
    ]
    for copy in lz_copies + sz_copies:
        copy.start()
    for copy in mix_copies:
        copy.wait_recv()
    mix = mix_buf[0]
    for h in range(1, HEADS):
        mix = mix + mix_buf[h]
    for i in range(3):
        mix_grad[i] = mix[:, i * DH : (i + 1) * DH]
    for copy in lz_copies:
        copy.wait_recv()
    slices = slice_z[z]
    for other in range(1, NZ):
        slices = slices + slice_z[lax.rem(z + NZ - other, NZ)]
    slice_all[y] = slices
    la_copies = [
        send(slice_all.at[y], slice_all.at[y], sem_la, k - 1, peer_y(z, y, k)) for k in (2, 1, 3)
    ]
    for copy in la_copies:
        copy.start()
    for copy in bz_copies:
        copy.wait_recv()
    total = big_stage[z]
    for k in range(NZ - 1):
        total = total + big_z[k]
    down_grad[...] = total[0:DH]
    for j in range(FF // D):
        up_grad[:, j * D : (j + 1) * D] = total[DH + 8 * j : DH + 8 * j + 8]
    out_grad[...] = total[2 * DH : BIG]
    for copy in sz_copies:
        copy.wait_recv()
    total = small_stage[z]
    for k in range(NZ - 1):
        total = total + small_z[k]
    feat_grad[...] = total[0:8]
    mid_grad[...] = total[8:16]
    for copy in la_copies:
        copy.wait_recv()
    slice_grad[...] = slice_all[...].reshape(DH, M)
    for copies in (
        mz_copies,
        my_copies,
        by_copies,
        g_copies,
        mix_copies,
        sy_copies,
        ly_copies,
        bz_copies,
        lz_copies,
        sz_copies,
        la_copies,
    ):
        for copy in copies:
            copy.wait_send()


def shape(dims, kind=F32):
    return jax.ShapeDtypeStruct(dims, kind)


def on_device(
    points,
    geometry,
    counts,
    cotangent,
    gain_attn,
    w_feat,
    w_mid,
    w_slice,
    sharpness,
    w_query,
    w_key,
    w_value,
    w_out,
    gain_mlp,
    w_up,
    w_down,
):
    vmem = pl.BlockSpec(memory_space=pltpu.VMEM)
    smem = pl.BlockSpec(memory_space=pltpu.SMEM)
    rows = 3 * RB

    def sems(count):
        return pltpu.SemaphoreType.DMA((2, count))

    first = pl.pallas_call(
        first_kernel,
        out_shape=(
            shape((rows, D), BF16),
            shape((rows, D), BF16),
            shape((rows, D), BF16),
            shape((HEADS, rows, M)),
            shape((HEADS, rows, M), BF16),
            shape((HEADS, D, M), BF16),
            shape((HEADS, DH, M)),
            shape((2 * M, M)),
            shape((DH, 2 * M)),
            shape((DH, M)),
            shape((2, DH, 2 * M)),
            shape((SUMS, M)),
        ),
        in_specs=[vmem, vmem, smem, vmem, vmem, vmem, vmem, smem, vmem, vmem, vmem],
        out_specs=(vmem,) * 12,
        scratch_shapes=[
            pltpu.VMEM((HEADS, SUMS, M), F32),
            pltpu.VMEM((NZ - 1, SUMS, M), F32),
            pltpu.VMEM((NY, SUMS, M), F32),
            pltpu.VMEM((HEADS, DH, M), F32),
            pltpu.VMEM((D, rows), BF16),
            sems(NZ - 1),
            sems(NY - 1),
            sems(NZ - 1),
        ],
        compiler_params=pltpu.CompilerParams(
            collective_id=0, has_side_effects=True, vmem_limit_bytes=VMEM_BYTES
        ),
        name="slice_sums_and_mixing",
    )
    gain_row = gain_attn.reshape(1, D)
    normed, feats, mids, shares, wlow, wsm, mixed, attn, both, query, keyval, sums = first(
        points, geometry, counts, gain_row, w_feat, w_mid, w_slice, sharpness, w_query, w_key, w_value
    )
    second = pl.pallas_call(
        second_kernel,
        out_shape=(
            shape((RB, D), BF16),
            shape((8, D)),
            shape((8, D)),
            shape((8, D)),
            shape((8, FF)),
            shape((DH, D)),
            shape((DH, M)),
            shape((3, DH, DH)),
        ),
        in_specs=[vmem, vmem, smem] + [vmem] * 12 + [smem] + [vmem] * 7,
        out_specs=(vmem,) * 8,
        scratch_shapes=[
            pltpu.VMEM((HEADS, D, M), BF16),
            pltpu.VMEM((HEADS, D, M), BF16),
            pltpu.VMEM((HEADS, D, M), BF16),
            pltpu.VMEM((RB, D), BF16),
            pltpu.VMEM((RB, FF), BF16),
            pltpu.VMEM((RB, FF), BF16),
            pltpu.VMEM((RB, D), F32),
            pltpu.VMEM((RB, D), BF16),
            pltpu.VMEM((RB, D), BF16),
            pltpu.VMEM((RB, D), BF16),
            pltpu.VMEM((D, rows), BF16),
            pltpu.VMEM((D, rows), BF16),
            pltpu.VMEM((rows, D), F32),
            pltpu.VMEM((rows, D), F32),
            pltpu.VMEM((HEADS, DH, M), F32),
            pltpu.VMEM((NZ - 1, DH, M), F32),
            pltpu.VMEM((NY, DH, M), F32),
            pltpu.VMEM((HEADS, SUMS, M), F32),
            pltpu.VMEM((HEADS, DH, 4 * DH), F32),
            pltpu.VMEM((NZ, NY, BIG, D), F32),
            pltpu.VMEM((NY - 1, NZ, BIG, D), F32),
            pltpu.VMEM((NZ, BIG, D), F32),
            pltpu.VMEM((NZ - 1, BIG, D), F32),
            pltpu.VMEM((NZ, NY, SMALL, D), F32),
            pltpu.VMEM((NY - 1, NZ, SMALL, D), F32),
            pltpu.VMEM((NZ, SMALL, D), F32),
            pltpu.VMEM((NZ - 1, SMALL, D), F32),
            pltpu.VMEM((NY, 8, M), F32),
            pltpu.VMEM((NY - 1, 8, M), F32),
            pltpu.VMEM((NZ, 8, M), F32),
            pltpu.VMEM((NY, 8, M), F32),
            sems(NZ - 1),
            sems(NY - 1),
            sems(NZ - 1),
            sems(NZ - 1),
            sems(NY - 1),
            sems(NZ - 1),
            sems(NY - 1),
            sems(NZ - 1),
            sems(NY - 1),
            sems(NZ - 1),
            sems(NY - 1),
        ],
        compiler_params=pltpu.CompilerParams(
            collective_id=1, has_side_effects=True, vmem_limit_bytes=VMEM_BYTES
        ),
        name="mlp_and_backward",
    )
    return second(
        points,
        cotangent,
        counts,
        wlow,
        shares,
        normed,
        feats,
        mids,
        wsm,
        mixed,
        attn,
        both,
        query,
        keyval,
        sums,
        sharpness,
        gain_mlp.reshape(1, D),
        w_out,
        w_up,
        w_down,
        w_query,
        w_key,
        w_value,
    )


def solution(mesh):
    rows = P(("design", "pts"), None)
    return jax.shard_map(
        on_device,
        mesh=mesh,
        in_specs=(rows, rows, P(("design", "pts")), rows) + (P(),) * 12,
        out_specs=(rows,) * 6 + (P("design", None), P("design", None, None)),
        check_vma=False,
    )
```

```python
import math

import jax
import jax.numpy as jnp
from jax import lax
from jax.experimental import pallas as pl
from jax.experimental.pallas import tpu as pltpu
from jax.sharding import PartitionSpec as P

F32 = jnp.float32
BF16 = jnp.bfloat16
HIGH = lax.Precision.HIGHEST
NY = 4
NZ = 8
HEADS = 8
DH = 32
M = 256
D = 256
FF = 1024
RB = 256
SUMS = 72
BIG = 40
SMALL = 16
ROWS = 120
EPS = 1e-05
VMEM_BYTES = 64000000
ORDER = (4, 3, 5, 2, 6, 1, 7)


def nn(a, b, precision=None):
    return lax.dot_general(
        a, b, (((1,), (0,)), ((), ())), precision=precision, preferred_element_type=F32
    )


def nt(a, b, precision=None):
    return lax.dot_general(
        a, b, (((1,), (1,)), ((), ())), precision=precision, preferred_element_type=F32
    )


def tn(a, b, precision=None):
    return lax.dot_general(
        a, b, (((0,), (0,)), ((), ())), precision=precision, preferred_element_type=F32
    )


def norm_parts(x):
    centre = jnp.mean(x, axis=-1, keepdims=True)
    shifted = x - centre
    spread = jnp.mean(shifted * shifted, axis=-1, keepdims=True)
    scale = lax.rsqrt(spread + EPS)
    return shifted * scale, scale


def place():
    me = lax.axis_index("pts")
    return lax.div(me, NY), lax.rem(me, NY)


def peer_z(z, y, k):
    return {"pts": lax.rem(z + k, NZ) * NY + y}


def peer_y(z, y, k):
    return {"pts": z * NY + lax.rem(y + k, NY)}


def greet(z, y):
    barrier = pltpu.get_barrier_semaphore()
    for k in range(1, NZ):
        pl.semaphore_signal(barrier, inc=1, device_id=peer_z(z, y, k), device_id_type=pl.DeviceIdType.MESH)
    for k in range(1, NY):
        pl.semaphore_signal(barrier, inc=1, device_id=peer_y(z, y, k), device_id_type=pl.DeviceIdType.MESH)


def meet():
    pl.semaphore_wait(pltpu.get_barrier_semaphore(), NZ - 1 + NY - 1)


def send(src, dst, sems, slot, device):
    return pltpu.make_async_remote_copy(
        src_ref=src,
        dst_ref=dst,
        send_sem=sems.at[0, slot],
        recv_sem=sems.at[1, slot],
        device_id=device,
        device_id_type=pl.DeviceIdType.MESH,
    )


def swing(k):
    return 4 + (1 - 2 * lax.rem(k, 2)) * lax.div(k + 1, 2)


def layer_kernel(
    points,
    geometry,
    cotangent,
    counts,
    sharp,
    gain_attn,
    gain_mlp,
    w_feat,
    w_mid,
    w_slice,
    w_query,
    w_key,
    w_value,
    w_out,
    w_up,
    w_down,
    layer_out,
    packed,
    mix_grad,
    normed_t,
    feats,
    feat_t,
    mids,
    mid_t,
    shares,
    wlow,
    wsm,
    mixm,
    num_m,
    geo_m,
    grad_hid,
    low_up,
    grad_up_low,
    att_rows,
    res_rows,
    att_grad,
    acc_feat,
    acc_mid,
    part,
    zbuf,
    ybuf,
    mbuf,
    mg_part,
    mg_z,
    mg_y,
    gbuf,
    mix_buf,
    down,
    down_y,
    down_stage,
    down_z,
    big,
    big_y,
    big_stage,
    big_z,
    small,
    small_y,
    small_stage,
    small_z,
    slice_part,
    slice_y,
    slice_z,
    slice_all,
    sem_z,
    sem_y,
    sem_m,
    sem_mz,
    sem_my,
    sem_g,
    sem_mix,
    sem_dy,
    sem_dz,
    sem_by,
    sem_bz,
    sem_sy,
    sem_sz,
    sem_ly,
    sem_lz,
    sem_la,
):
    z, y = place()
    greet(z, y)
    wsm[...] = jnp.zeros_like(wsm)
    for h in range(HEADS):
        wsm[h, h * DH : (h + 1) * DH, :] = w_slice[...]
    for b in range(3):
        rows = slice(b * RB, (b + 1) * RB)
        x = points[...] if b == 0 else geometry[(b - 1) * RB : b * RB, :]
        normed = norm_parts(x.astype(F32))[0] * gain_attn[...]
        normed_t[:, rows] = normed.T.astype(BF16)
        normed = normed.astype(BF16)
        found = nn(normed, w_feat[...])
        feats[rows, :] = found.astype(BF16)
        feat_t[:, rows] = found.T.astype(BF16)
        mids[rows, :] = nn(normed, w_mid[...]).astype(BF16)
    live = lax.broadcasted_iota(jnp.int32, (RB, 1), 0) < counts[0]
    valid = jnp.where(live, 1.0, 0.0).astype(F32)
    pick = lax.broadcasted_iota(jnp.int32, (8, M), 0)
    meet()

    def sums_step(k, carry):
        h = lax.rem(z + swing(k), NZ)
        weight = wsm[h]
        factor = sharp[h]
        row = pl.multiple_of(h * DH, DH)
        numers = []
        denoms = []
        for b in range(3):
            rows = slice(b * RB, (b + 1) * RB)
            logits = nn(mids[rows, :], weight) * factor
            powers = jnp.exp(logits - jnp.max(logits, axis=-1, keepdims=True))
            share = powers * (1.0 / jnp.sum(powers, axis=-1, keepdims=True))
            shares[h, rows, :] = share
            weights = share * valid if b == 0 else share
            low = weights.astype(BF16)
            wlow[h, rows, :] = low
            denoms.append(jnp.sum(weights, axis=0, keepdims=True))
            numers.append(nn(feat_t[pl.ds(row, DH), rows], low))
        part[h, 0:DH, :] = numers[0]
        part[h, DH : 2 * DH, :] = numers[1] + numers[2]
        part[h, 2 * DH : SUMS, :] = jnp.where(
            pick == 0, denoms[0], jnp.where(pick == 1, denoms[1] + denoms[2], 0.0)
        )

        @pl.when(k < NZ - 1)
        def _():
            send(part.at[h], zbuf.at[k], sem_z, k, peer_z(z, y, swing(k))).start()

        return carry

    lax.fori_loop(0, NZ, sums_step, 0)
    for b in range(3):
        rows = slice(b * RB, (b + 1) * RB)
        mid_t[:, rows] = mids[rows, :].astype(F32).T.astype(BF16)
    mixm[...] = jnp.zeros_like(mixm)
    num_m[...] = jnp.zeros_like(num_m)
    geo_m[...] = jnp.zeros_like(geo_m)
    z_copies = [
        send(part.at[lax.rem(z + k, NZ)], zbuf.at[i], sem_z, i, peer_z(z, y, k))
        for i, k in enumerate(ORDER)
    ]
    total = part[z]
    for i in range(NZ - 1):
        z_copies[i].wait_recv()
        total = total + zbuf[i]
    ybuf[0] = total
    y_copies = [send(ybuf.at[0], ybuf.at[k], sem_y, k - 1, peer_y(z, y, k)) for k in (2, 1, 3)]
    for copy in y_copies:
        copy.start()
    acc_feat[...] = jnp.zeros_like(acc_feat)
    acc_mid[...] = jnp.zeros_like(acc_mid)
    slice_part[...] = jnp.zeros_like(slice_part)
    for copy in y_copies:
        copy.wait_recv()
    sums = ybuf[y]
    for other in range(1, NY):
        sums = sums + ybuf[lax.rem(y + NY - other, NY)]
    den = sums[2 * DH : 2 * DH + 1] + EPS
    geo_den = sums[2 * DH + 1 : 2 * DH + 2] + EPS
    field = sums[0:DH] / den
    both = jnp.concatenate([field, sums[DH : 2 * DH] / geo_den], axis=1)
    query = tn(w_query[...], field, HIGH)
    keys = tn(w_key[...], both, HIGH)
    values = tn(w_value[...], both, HIGH)
    scores = tn(keys, query, HIGH) * (1.0 / math.sqrt(DH))
    powers = jnp.exp(scores - jnp.max(scores, axis=0, keepdims=True))
    attention = powers * (1.0 / jnp.sum(powers, axis=0, keepdims=True))
    mbuf[z] = nn(values, attention, HIGH)
    m_copies = [send(mbuf.at[z], mbuf.at[z], sem_m, k - 1, peer_z(z, y, k)) for k in ORDER]
    for copy in m_copies:
        copy.start()
    for j in range(FF // D):
        cols = slice(j * D, (j + 1) * D)
        grad_hid[:, cols] = nt(cotangent[...], w_down[cols, :])
    for copy in m_copies:
        copy.wait_recv()
    for h in range(HEADS):
        mixm[h, h * DH : (h + 1) * DH, :] = mbuf[h].astype(BF16)
    attended = nt(wlow[0, 0:RB, :], mixm[0])
    for h in range(1, HEADS):
        attended = attended + nt(wlow[h, 0:RB, :], mixm[h])
    attended = attended.astype(BF16)
    att_rows[...] = attended
    residual = points[...].astype(F32) + nn(attended, w_out[...])
    hat, scale = norm_parts(residual)
    second_low = (hat * gain_mlp[...]).astype(BF16)
    low_up[...] = second_low
    const = math.sqrt(2.0 / math.pi)
    layer = residual
    grad_second = jnp.zeros((RB, D), F32)
    for j in range(FF // D):
        cols = slice(j * D, (j + 1) * D)
        upper = nn(second_low, w_up[:, cols])
        square = upper * upper
        tanh = jnp.tanh(const * upper * (1.0 + 0.044715 * square))
        half = 0.5 * (1.0 + tanh)
        hidden = upper * half
        down[2 * j : 2 * j + 2] = nn(hidden.T.astype(BF16), cotangent[...]).reshape(2, NY, DH, D)
        layer = layer + nn(hidden.astype(BF16), w_down[cols, :])
        slope = half + 0.5 * upper * (1.0 - tanh * tanh) * (const * (1.0 + 3.0 * 0.044715 * square))
        grad_upper = (grad_hid[:, cols] * slope).astype(BF16)
        grad_up_low[:, cols] = grad_upper
        grad_second = grad_second + nt(grad_upper, w_up[:, cols])
    dy_copies = [
        send(down.at[:, lax.rem(y + k, NY)], down_y.at[k - 1], sem_dy, k - 1, peer_y(z, y, k))
        for k in (2, 1, 3)
    ]
    for copy in dy_copies:
        copy.start()
    layer_out[...] = layer.astype(BF16)
    scaled = grad_second * gain_mlp[...]
    back = scale * (
        scaled
        - jnp.mean(scaled, axis=-1, keepdims=True)
        - hat * jnp.mean(scaled * hat, axis=-1, keepdims=True)
    )
    grad_resid = (cotangent[...].astype(F32) + back).astype(BF16)
    res_rows[...] = grad_resid
    grad_att = nt(grad_resid, w_out[...])
    att_grad[...] = grad_att.astype(BF16)
    att_t = grad_att.T.astype(BF16)
    for h in range(HEADS):
        mg_part[h] = nn(att_t[h * DH : (h + 1) * DH, :], wlow[h, 0:RB, :])
    mz_copies = [
        send(mg_part.at[lax.rem(z + k, NZ)], mg_z.at[k - 1], sem_mz, k - 1, peer_z(z, y, k))
        for k in ORDER
    ]
    for copy in mz_copies:
        copy.start()
    low_up_t = low_up[...].astype(F32).T.astype(BF16)
    for j in range(FF // D):
        up = nn(low_up_t, grad_up_low[:, j * D : (j + 1) * D])
        big[:, :, 8 * j : 8 * j + 8, :] = up.reshape(NZ, NY, 8, D)
    out = nn(att_rows[...].astype(F32).T.astype(BF16), res_rows[...])
    big[:, :, DH:BIG, :] = out.reshape(NZ, NY, 8, D)
    for copy in mz_copies:
        copy.wait_recv()
    total = mg_part[z]
    for k in range(NZ - 1):
        total = total + mg_z[k]
    mg_y[0] = total
    my_copies = [
        send(mg_y.at[0], mg_y.at[k], sem_my, k - 1, peer_y(z, y, k)) for k in (2, 1, 3)
    ]
    for copy in my_copies:
        copy.start()
    by_copies = [
        send(big.at[:, lax.rem(y + k, NY)], big_y.at[k - 1], sem_by, k - 1, peer_y(z, y, k))
        for k in (2, 1, 3)
    ]
    for copy in by_copies:
        copy.start()
    for copy in dy_copies:
        copy.wait_recv()
    down_stage[...] = ((down[:, y] + down_y[0]) + down_y[1]) + down_y[2]
    dz_copies = [
        send(down_stage.at[lax.rem(z + k, NZ)], down_z.at[k - 1], sem_dz, k - 1, peer_z(z, y, k))
        for k in ORDER
    ]
    for copy in dz_copies:
        copy.start()
    for copy in my_copies:
        copy.wait_recv()
    grad = mg_y[y]
    for other in range(1, NY):
        grad = grad + mg_y[lax.rem(y + NY - other, NY)]
    d_value = nt(grad, attention, HIGH)
    d_attn = tn(values, grad, HIGH)
    inner = jnp.sum(attention * d_attn, axis=0, keepdims=True)
    d_score = attention * (d_attn - inner) * (1.0 / math.sqrt(DH))
    d_query = nn(keys, d_score, HIGH)
    d_key = nt(query, d_score, HIGH)
    d_both = nn(w_key[...], d_key, HIGH) + nn(w_value[...], d_value, HIGH)
    d_field = (d_both[:, 0:M] + nn(w_query[...], d_query, HIGH)) / den
    d_geo = d_both[:, M : 2 * M] / geo_den
    gbuf[z, 0:DH, :] = d_field
    gbuf[z, DH : 2 * DH, :] = d_geo
    den_grad = -jnp.sum(d_field * both[:, 0:M], axis=0, keepdims=True)
    geo_den_grad = -jnp.sum(d_geo * both[:, M : 2 * M], axis=0, keepdims=True)
    gbuf[z, 2 * DH : SUMS, :] = jnp.where(pick == 0, den_grad, jnp.where(pick == 1, geo_den_grad, 0.0))
    g_copies = [
        send(gbuf.at[z], gbuf.at[z], sem_g, i, peer_z(z, y, k)) for i, k in enumerate(ORDER)
    ]
    for copy in g_copies:
        copy.start()
    mix_buf[z, :, 0:DH] = nt(field, d_query, HIGH)
    mix_buf[z, :, DH : 2 * DH] = nt(both, d_key, HIGH)
    mix_buf[z, :, 2 * DH : 3 * DH] = nt(both, d_value, HIGH)
    mix_buf[z, :, 3 * DH : 4 * DH] = jnp.zeros((DH, DH), F32)
    mix_copies = [
        send(mix_buf.at[z], mix_buf.at[z], sem_mix, k - 1, peer_z(z, y, k)) for k in ORDER
    ]
    for copy in mix_copies:
        copy.start()

    def back_step(k, carry):
        away = lax.rem(swing(lax.rem(k + NZ - 1, NZ)), NZ)
        h = lax.rem(z + NZ - away, NZ)

        @pl.when(k > 0)
        def _():
            send(gbuf.at[z], gbuf.at[h], sem_g, k - 1, peer_z(z, y, away)).wait_recv()

        row = pl.multiple_of(h * DH, DH)
        num_m[h, pl.ds(row, DH), :] = gbuf[h, 0:DH, :].astype(BF16)
        geo_m[h, pl.ds(row, DH), :] = gbuf[h, DH : 2 * DH, :].astype(BF16)
        factor = sharp[h]
        for b in range(3):
            rows = slice(b * RB, (b + 1) * RB)
            token = num_m[h] if b == 0 else geo_m[h]
            grad_w = nn(feats[rows, :], token)
            if b == 0:
                grad_w = grad_w + nn(att_grad[...], mixm[h])
                grad_w = (grad_w + gbuf[h, 2 * DH : 2 * DH + 1, :]) * valid
            else:
                grad_w = grad_w + gbuf[h, 2 * DH + 1 : 2 * DH + 2, :]
            share = shares[h, rows, :]
            inside = jnp.sum(share * grad_w, axis=-1, keepdims=True)
            low = (share * (grad_w - inside) * factor).astype(BF16)
            slice_part[...] += nn(mid_t[pl.ds(row, DH), rows], low).reshape(NY, 8, M)
            acc_mid[rows, :] += nt(low, wsm[h])
            acc_feat[rows, :] += nt(wlow[h, rows, :], token)
        return carry

    lax.fori_loop(0, NZ, back_step, 0)
    feat_total = nn(normed_t[...], acc_feat[...].astype(BF16))
    small[:, :, 0:8, :] = feat_total.reshape(NZ, NY, 8, D)
    mid_total = nn(normed_t[...], acc_mid[...].astype(BF16))
    small[:, :, 8:16, :] = mid_total.reshape(NZ, NY, 8, D)
    ly_copies = [
        send(slice_part.at[lax.rem(y + k, NY)], slice_y.at[k - 1], sem_ly, k - 1, peer_y(z, y, k))
        for k in (2, 1, 3)
    ]
    sy_copies = [
        send(small.at[:, lax.rem(y + k, NY)], small_y.at[k - 1], sem_sy, k - 1, peer_y(z, y, k))
        for k in (2, 1, 3)
    ]
    for copy in ly_copies + sy_copies:
        copy.start()
    for copy in by_copies:
        copy.wait_recv()
    big_stage[...] = ((big[:, y] + big_y[0]) + big_y[1]) + big_y[2]
    bz_copies = [
        send(big_stage.at[lax.rem(z + k, NZ)], big_z.at[k - 1], sem_bz, k - 1, peer_z(z, y, k))
        for k in ORDER
    ]
    for copy in ly_copies:
        copy.wait_recv()
    slice_z[0] = ((slice_part[y] + slice_y[0]) + slice_y[1]) + slice_y[2]
    lz_copies = [send(slice_z.at[0], slice_z.at[k], sem_lz, k - 1, peer_z(z, y, k)) for k in ORDER]
    for copy in lz_copies + bz_copies:
        copy.start()
    for copy in dz_copies:
        copy.wait_recv()
    total = down_stage[z]
    for k in range(NZ - 1):
        total = total + down_z[k]
    packed[0:DH] = total
    for copy in mix_copies:
        copy.wait_recv()
    mix = mix_buf[0]
    for h in range(1, HEADS):
        mix = mix + mix_buf[h]
    for i in range(3):
        mix_grad[i] = mix[:, i * DH : (i + 1) * DH]
    for copy in sy_copies:
        copy.wait_recv()
    small_stage[...] = ((small[:, y] + small_y[0]) + small_y[1]) + small_y[2]
    sz_copies = [
        send(small_stage.at[lax.rem(z + k, NZ)], small_z.at[k - 1], sem_sz, k - 1, peer_z(z, y, k))
        for k in ORDER
    ]
    for copy in sz_copies:
        copy.start()
    for copy in lz_copies:
        copy.wait_recv()
    slices = slice_z[z]
    for other in range(1, NZ):
        slices = slices + slice_z[lax.rem(z + NZ - other, NZ)]
    slice_all[y] = slices
    la_copies = [
        send(slice_all.at[y], slice_all.at[y], sem_la, k - 1, peer_y(z, y, k)) for k in (2, 1, 3)
    ]
    for copy in la_copies:
        copy.start()
    for copy in bz_copies:
        copy.wait_recv()
    total = big_stage[z]
    for k in range(NZ - 1):
        total = total + big_z[k]
    packed[DH : DH + BIG] = total
    for copy in la_copies:
        copy.wait_recv()
    packed[DH + BIG + SMALL : ROWS] = slice_all[...].reshape(DH, M)
    for copy in sz_copies:
        copy.wait_recv()
    total = small_stage[z]
    for k in range(NZ - 1):
        total = total + small_z[k]
    packed[DH + BIG : DH + BIG + SMALL] = total
    for copies in (
        z_copies,
        y_copies,
        m_copies,
        dy_copies,
        dz_copies,
        mz_copies,
        my_copies,
        by_copies,
        g_copies,
        mix_copies,
        sy_copies,
        ly_copies,
        bz_copies,
        lz_copies,
        sz_copies,
        la_copies,
    ):
        for copy in copies:
            copy.wait_send()


def result_kernel(
    layer_in,
    packed,
    mix_in,
    layer_out,
    feat_grad,
    mid_grad,
    out_grad,
    up_grad,
    down_grad,
    slice_grad,
    mix_grad,
):
    layer_out[...] = layer_in[...]
    down_grad[...] = packed[0:DH]
    for j in range(FF // D):
        up_grad[:, j * D : (j + 1) * D] = packed[DH + 8 * j : DH + 8 * j + 8]
    out_grad[...] = packed[2 * DH : 2 * DH + 8]
    feat_grad[...] = packed[2 * DH + 8 : 2 * DH + 16]
    mid_grad[...] = packed[2 * DH + 16 : 2 * DH + 24]
    slice_grad[...] = packed[2 * DH + 24 : ROWS]
    mix_grad[...] = mix_in[...]


def shape(dims, kind=F32):
    return jax.ShapeDtypeStruct(dims, kind)


def on_device(
    points,
    geometry,
    counts,
    cotangent,
    gain_attn,
    w_feat,
    w_mid,
    w_slice,
    sharpness,
    w_query,
    w_key,
    w_value,
    w_out,
    gain_mlp,
    w_up,
    w_down,
):
    vmem = pl.BlockSpec(memory_space=pltpu.VMEM)
    smem = pl.BlockSpec(memory_space=pltpu.SMEM)
    rows = 3 * RB

    def held(*dims):
        return pltpu.VMEM(dims, F32)

    def low(*dims):
        return pltpu.VMEM(dims, BF16)

    along_z = pltpu.SemaphoreType.DMA((2, NZ - 1))
    along_y = pltpu.SemaphoreType.DMA((2, NY - 1))
    layer, packed, mix = pl.pallas_call(
        layer_kernel,
        out_shape=(shape((RB, D), BF16), shape((ROWS, D)), shape((3, DH, DH))),
        in_specs=[vmem] * 3 + [smem] * 2 + [vmem] * 11,
        out_specs=(vmem,) * 3,
        scratch_shapes=[
            low(D, rows),
            low(rows, D),
            low(D, rows),
            low(rows, D),
            low(D, rows),
            held(HEADS, rows, M),
            low(HEADS, rows, M),
            low(HEADS, D, M),
            low(HEADS, D, M),
            low(HEADS, D, M),
            low(HEADS, D, M),
            held(RB, FF),
            low(RB, D),
            low(RB, FF),
            low(RB, D),
            low(RB, D),
            low(RB, D),
            held(rows, D),
            held(rows, D),
            held(HEADS, SUMS, M),
            held(NZ - 1, SUMS, M),
            held(NY, SUMS, M),
            held(HEADS, DH, M),
            held(HEADS, DH, M),
            held(NZ - 1, DH, M),
            held(NY, DH, M),
            held(HEADS, SUMS, M),
            held(HEADS, DH, 4 * DH),
            held(NZ, NY, DH, D),
            held(NY - 1, NZ, DH, D),
            held(NZ, DH, D),
            held(NZ - 1, DH, D),
            held(NZ, NY, BIG, D),
            held(NY - 1, NZ, BIG, D),
            held(NZ, BIG, D),
            held(NZ - 1, BIG, D),
            held(NZ, NY, SMALL, D),
            held(NY - 1, NZ, SMALL, D),
            held(NZ, SMALL, D),
            held(NZ - 1, SMALL, D),
            held(NY, 8, M),
            held(NY - 1, 8, M),
            held(NZ, 8, M),
            held(NY, 8, M),
            along_z,
            along_y,
            along_z,
            along_z,
            along_y,
            along_z,
            along_z,
            along_y,
            along_z,
            along_y,
            along_z,
            along_y,
            along_z,
            along_y,
            along_z,
            along_y,
        ],
        compiler_params=pltpu.CompilerParams(
            collective_id=0, has_side_effects=True, vmem_limit_bytes=VMEM_BYTES
        ),
        name="layer",
    )(
        points,
        geometry,
        cotangent,
        counts,
        sharpness,
        gain_attn.reshape(1, D),
        gain_mlp.reshape(1, D),
        w_feat,
        w_mid,
        w_slice,
        w_query,
        w_key,
        w_value,
        w_out,
        w_up,
        w_down,
    )
    return pl.pallas_call(
        result_kernel,
        out_shape=(
            shape((RB, D), BF16),
            shape((8, D)),
            shape((8, D)),
            shape((8, D)),
            shape((8, FF)),
            shape((DH, D)),
            shape((DH, M)),
            shape((3, DH, DH)),
        ),
        in_specs=[vmem] * 3,
        out_specs=(vmem,) * 8,
        name="results",
    )(layer, packed, mix)


def solution(mesh):
    rows = P(("design", "pts"), None)
    return jax.shard_map(
        on_device,
        mesh=mesh,
        in_specs=(rows, rows, P(("design", "pts")), rows) + (P(),) * 12,
        out_specs=(rows,) * 6 + (P("design", None), P("design", None, None)),
        check_vma=False,
    )
```

```python
import math

import jax
import jax.numpy as jnp
from jax import lax
from jax.experimental import pallas as pl
from jax.experimental.pallas import tpu as pltpu
from jax.sharding import PartitionSpec as P

F32 = jnp.float32
BF16 = jnp.bfloat16
HIGH = lax.Precision.HIGHEST
NY = 4
NZ = 8
HEADS = 8
DH = 32
M = 256
D = 256
FF = 1024
RB = 256
SUMS = 72
BIG = 40
SMALL = 16
ROWS = 120
CUT = 40
EPS = 1e-05
VMEM_BYTES = 64000000
ORDER = (4, 3, 5, 2, 6, 1, 7)


def nn(a, b, precision=None):
    return lax.dot_general(
        a, b, (((1,), (0,)), ((), ())), precision=precision, preferred_element_type=F32
    )


def nt(a, b, precision=None):
    return lax.dot_general(
        a, b, (((1,), (1,)), ((), ())), precision=precision, preferred_element_type=F32
    )


def tn(a, b, precision=None):
    return lax.dot_general(
        a, b, (((0,), (0,)), ((), ())), precision=precision, preferred_element_type=F32
    )


def split(x):
    high = x.astype(BF16)
    return high, (x - high.astype(F32)).astype(BF16)


def wide(product, a, b):
    a_high, a_low = split(a)
    b_high, b_low = split(b)
    return product(a_high, b_high) + (product(a_low, b_high) + product(a_high, b_low))


def wide_tn(a, b):
    a_high, a_low = split(a)
    b_high, b_low = split(b)
    return tn(
        jnp.concatenate([a_high, a_low, a_high], axis=0),
        jnp.concatenate([b_high, b_high, b_low], axis=0),
    )


def norm_parts(x):
    centre = jnp.mean(x, axis=-1, keepdims=True)
    shifted = x - centre
    spread = jnp.mean(shifted * shifted, axis=-1, keepdims=True)
    scale = lax.rsqrt(spread + EPS)
    return shifted * scale, scale


def place():
    me = lax.axis_index("pts")
    return lax.div(me, NY), lax.rem(me, NY)


def peer_z(z, y, k):
    return {"pts": lax.rem(z + k, NZ) * NY + y}


def peer_y(z, y, k):
    return {"pts": z * NY + lax.rem(y + k, NY)}


def greet(z, y):
    barrier = pltpu.get_barrier_semaphore()
    for k in range(1, NZ):
        pl.semaphore_signal(barrier, inc=1, device_id=peer_z(z, y, k), device_id_type=pl.DeviceIdType.MESH)
    for k in range(1, NY):
        pl.semaphore_signal(barrier, inc=1, device_id=peer_y(z, y, k), device_id_type=pl.DeviceIdType.MESH)


def meet():
    pl.semaphore_wait(pltpu.get_barrier_semaphore(), NZ - 1 + NY - 1)


def send(src, dst, sems, slot, device):
    return pltpu.make_async_remote_copy(
        src_ref=src,
        dst_ref=dst,
        send_sem=sems.at[0, slot],
        recv_sem=sems.at[1, slot],
        device_id=device,
        device_id_type=pl.DeviceIdType.MESH,
    )


def swing(k):
    return 4 + (1 - 2 * lax.rem(k, 2)) * lax.div(k + 1, 2)


def layer_kernel(
    points,
    geometry,
    cotangent,
    counts,
    sharp,
    gain_attn,
    gain_mlp,
    w_feat,
    w_mid,
    w_slice,
    w_query,
    w_key,
    w_value,
    w_out,
    w_up,
    w_down,
    layer_out,
    packed,
    mix_grad,
    normed_t,
    feats,
    feat_t,
    mids,
    mid_t,
    shares,
    wlow,
    wsm,
    mixm,
    num_m,
    geo_m,
    grad_hid,
    low_hidden,
    low_up,
    low_up_t,
    grad_up_low,
    att_rows,
    res_rows,
    att_grad,
    res_hold,
    acc_feat,
    acc_mid,
    both_in,
    attn,
    d_scores,
    mg_sum,
    part,
    zbuf,
    ybuf,
    mbuf,
    mg_part,
    mg_z,
    mg_y,
    gbuf,
    mix_buf,
    down,
    down_y,
    down_stage,
    down_z,
    big,
    big_y,
    big_stage,
    big_z,
    small,
    small_y,
    small_stage,
    small_z,
    slice_part,
    slice_y,
    slice_z,
    slice_all,
    sem_z,
    sem_y,
    sem_m,
    sem_mz,
    sem_my,
    sem_g,
    sem_mix,
    sem_dy,
    sem_dz,
    sem_by,
    sem_bz,
    sem_sy,
    sem_sz,
    sem_ly,
    sem_lz,
    sem_la,
):
    z, y = place()
    greet(z, y)
    wsm[...] = jnp.zeros_like(wsm)
    for h in range(HEADS):
        wsm[h, h * DH : (h + 1) * DH, :] = w_slice[...]
    for b in range(3):
        rows = slice(b * RB, (b + 1) * RB)
        x = points[...] if b == 0 else geometry[(b - 1) * RB : b * RB, :]
        normed = norm_parts(x.astype(F32))[0] * gain_attn[...]
        normed_t[:, rows] = normed.T.astype(BF16)
        normed = normed.astype(BF16)
        found = nn(normed, w_feat[...])
        feats[rows, :] = found.astype(BF16)
        feat_t[:, rows] = found.T.astype(BF16)
        mids[rows, :] = nn(normed, w_mid[...]).astype(BF16)
    live = lax.broadcasted_iota(jnp.int32, (RB, 1), 0) < counts[0]
    valid = jnp.where(live, 1.0, 0.0).astype(F32)
    pick = lax.broadcasted_iota(jnp.int32, (8, M), 0)
    key_query = nt(w_key[...], w_query[...], HIGH) * (1.0 / math.sqrt(DH))
    meet()

    def sums_step(k, carry):
        h = lax.rem(z + swing(k), NZ)
        weight = wsm[h]
        factor = sharp[h]
        row = pl.multiple_of(h * DH, DH)
        numers = []
        denoms = []
        for b in range(3):
            rows = slice(b * RB, (b + 1) * RB)
            logits = nn(mids[rows, :], weight) * factor
            powers = jnp.exp(logits - jnp.max(logits, axis=-1, keepdims=True))
            share = powers * (1.0 / jnp.sum(powers, axis=-1, keepdims=True))
            shares[h, rows, :] = share
            weights = share * valid if b == 0 else share
            low = weights.astype(BF16)
            wlow[h, rows, :] = low
            denoms.append(jnp.sum(weights, axis=0, keepdims=True))
            numers.append(nn(feat_t[pl.ds(row, DH), rows], low))
        part[h, 0:DH, :] = numers[0]
        part[h, DH : 2 * DH, :] = numers[1] + numers[2]
        part[h, 2 * DH : SUMS, :] = jnp.where(
            pick == 0, denoms[0], jnp.where(pick == 1, denoms[1] + denoms[2], 0.0)
        )

        @pl.when(k < NZ - 1)
        def _():
            send(part.at[h], zbuf.at[k], sem_z, k, peer_z(z, y, swing(k))).start()

        return carry

    lax.fori_loop(0, NZ, sums_step, 0)
    for b in range(3):
        rows = slice(b * RB, (b + 1) * RB)
        mid_t[:, rows] = mids[rows, :].astype(F32).T.astype(BF16)
    mixm[...] = jnp.zeros_like(mixm)
    num_m[...] = jnp.zeros_like(num_m)
    geo_m[...] = jnp.zeros_like(geo_m)
    z_copies = [
        send(part.at[lax.rem(z + k, NZ)], zbuf.at[i], sem_z, i, peer_z(z, y, k))
        for i, k in enumerate(ORDER)
    ]
    total = part[z]
    for i in range(NZ - 1):
        z_copies[i].wait_recv()
        total = total + zbuf[i]
    ybuf[0] = total
    y_copies = [send(ybuf.at[0], ybuf.at[k], sem_y, k - 1, peer_y(z, y, k)) for k in (2, 1, 3)]
    for copy in y_copies:
        copy.start()
    slice_part[...] = jnp.zeros_like(slice_part)
    for copy in y_copies:
        copy.wait_recv()
    sums = ybuf[y]
    for other in range(1, NY):
        sums = sums + ybuf[lax.rem(y + NY - other, NY)]
    den = sums[2 * DH : 2 * DH + 1] + EPS
    geo_den = sums[2 * DH + 1 : 2 * DH + 2] + EPS
    field = sums[0:DH] / den
    both = jnp.concatenate([field, sums[DH : 2 * DH] / geo_den], axis=1)
    both_in[...] = both
    query = wide(nn, key_query, field)
    values = wide(tn, w_value[...], both)
    scores = wide_tn(both, query)
    powers = jnp.exp(scores - jnp.max(scores, axis=0, keepdims=True))
    attention = powers * (1.0 / jnp.sum(powers, axis=0, keepdims=True))
    attn[...] = attention
    mbuf[z] = wide(nn, values, attention)
    m_copies = [send(mbuf.at[z], mbuf.at[z], sem_m, k - 1, peer_z(z, y, k)) for k in ORDER]
    for copy in m_copies:
        copy.start()
    for j in range(FF // D):
        cols = slice(j * D, (j + 1) * D)
        grad_hid[:, cols] = nt(cotangent[...], w_down[cols, :])
    key_side = wide(tn, key_query, both)
    for copy in m_copies:
        copy.wait_recv()
    for h in range(HEADS):
        mixm[h, h * DH : (h + 1) * DH, :] = mbuf[h].astype(BF16)
    attended = nt(wlow[0, 0:RB, :], mixm[0])
    for h in range(1, HEADS):
        attended = attended + nt(wlow[h, 0:RB, :], mixm[h])
    attended = attended.astype(BF16)
    att_rows[...] = attended
    residual = points[...].astype(F32) + nn(attended, w_out[...])
    hat, scale = norm_parts(residual)
    second_low = (hat * gain_mlp[...]).astype(BF16)
    low_up[...] = second_low
    const = math.sqrt(2.0 / math.pi)
    res_hold[...] = residual
    grad_second = jnp.zeros((RB, D), F32)
    for j in range(FF // D):
        cols = slice(j * D, (j + 1) * D)
        upper = nn(second_low, w_up[:, cols])
        square = upper * upper
        tanh = jnp.tanh(const * upper * (1.0 + 0.044715 * square))
        half = 0.5 * (1.0 + tanh)
        hidden = upper * half
        down[2 * j : 2 * j + 2] = nn(hidden.T.astype(BF16), cotangent[...]).reshape(2, NY, DH, D)
        low_hidden[:, cols] = hidden.astype(BF16)
        slope = half + 0.5 * upper * (1.0 - tanh * tanh) * (const * (1.0 + 3.0 * 0.044715 * square))
        grad_upper = (grad_hid[:, cols] * slope).astype(BF16)
        grad_up_low[:, cols] = grad_upper
        grad_second = grad_second + nt(grad_upper, w_up[:, cols])
    dy_copies = [
        send(down.at[:, lax.rem(y + k, NY)], down_y.at[k - 1], sem_dy, k - 1, peer_y(z, y, k))
        for k in (2, 1, 3)
    ]
    for copy in dy_copies:
        copy.start()
    scaled = grad_second * gain_mlp[...]
    back = scale * (
        scaled
        - jnp.mean(scaled, axis=-1, keepdims=True)
        - hat * jnp.mean(scaled * hat, axis=-1, keepdims=True)
    )
    grad_resid = (cotangent[...].astype(F32) + back).astype(BF16)
    res_rows[...] = grad_resid
    grad_att = nt(grad_resid, w_out[...])
    att_grad[...] = grad_att.astype(BF16)
    att_t = grad_att.T.astype(BF16)
    for h in range(HEADS):
        mg_part[h] = nn(att_t[h * DH : (h + 1) * DH, :], wlow[h, 0:RB, :])
    mz_copies = [
        send(mg_part.at[lax.rem(z + k, NZ)], mg_z.at[k - 1], sem_mz, k - 1, peer_z(z, y, k))
        for k in ORDER
    ]
    for copy in mz_copies:
        copy.start()
    low_up_t[...] = low_up[...].astype(F32).T.astype(BF16)

    def grads_step(j, carry):
        cols = pl.ds(pl.multiple_of(j * D, D), D)
        up = nn(low_up_t[...], grad_up_low[:, cols])
        big[:, :, pl.ds(pl.multiple_of(8 * j, 8), 8), :] = up.reshape(NZ, NY, 8, D)
        res_hold[...] += nn(low_hidden[:, cols], w_down[cols, :])
        return carry

    lax.fori_loop(0, FF // D, grads_step, 0)
    layer_out[...] = res_hold[...].astype(BF16)
    out = nn(att_rows[...].astype(F32).T.astype(BF16), res_rows[...])
    big[:, :, DH:BIG, :] = out.reshape(NZ, NY, 8, D)
    for copy in mz_copies:
        copy.wait_recv()
    total = mg_part[z]
    for k in range(NZ - 1):
        total = total + mg_z[k]
    mg_y[0] = total
    my_copies = [
        send(mg_y.at[0], mg_y.at[k], sem_my, k - 1, peer_y(z, y, k)) for k in (2, 1, 3)
    ]
    for copy in my_copies:
        copy.start()
    by_copies = [
        send(big.at[:, lax.rem(y + k, NY)], big_y.at[k - 1], sem_by, k - 1, peer_y(z, y, k))
        for k in (2, 1, 3)
    ]
    for copy in by_copies:
        copy.start()
    bz_copies = [
        send(big_stage.at[lax.rem(z + k, NZ)], big_z.at[k - 1], sem_bz, k - 1, peer_z(z, y, k))
        for k in ORDER
    ]
    for copy in dy_copies:
        copy.wait_recv()
    down_stage[...] = ((down[:, y] + down_y[0]) + down_y[1]) + down_y[2]
    dz_copies = [
        send(down_stage.at[lax.rem(z + k, NZ)], down_z.at[k - 1], sem_dz, k - 1, peer_z(z, y, k))
        for k in ORDER
    ]
    for copy in dz_copies:
        copy.start()
    for copy in my_copies:
        copy.wait_recv()
    grad = mg_y[y]
    for other in range(1, NY):
        grad = grad + mg_y[lax.rem(y + NY - other, NY)]
    mg_sum[...] = grad
    value_side = wide(nn, w_value[...], grad)
    d_attn = wide_tn(both, value_side)
    inner = jnp.sum(attention * d_attn, axis=0, keepdims=True)
    d_score = attention * (d_attn - inner)
    d_scores[...] = d_score
    d_both = wide(nt, query, d_score) + wide(nt, value_side, attention)
    d_field = (d_both[:, 0:M] + wide(nn, key_side, d_score)) / den
    d_geo = d_both[:, M : 2 * M] / geo_den
    den_grad = -jnp.sum(d_field * both[:, 0:M], axis=0, keepdims=True)
    geo_den_grad = -jnp.sum(d_geo * both[:, M : 2 * M], axis=0, keepdims=True)
    gbuf[z, 0:DH, :] = d_field
    gbuf[z, DH:CUT, :] = jnp.where(pick == 0, den_grad, jnp.where(pick == 1, geo_den_grad, 0.0))
    gbuf[z, CUT:SUMS, :] = d_geo

    def relay(step, way, half, origin):
        piece = gbuf.at[origin, half * CUT : CUT + half * DH]
        return pltpu.make_async_remote_copy(
            src_ref=piece,
            dst_ref=piece,
            send_sem=sem_g.at[0, way, half, step],
            recv_sem=sem_g.at[1, way, half, step],
            device_id=peer_z(z, y, 1 if way == 0 else NZ - 1),
            device_id_type=pl.DeviceIdType.MESH,
        )

    for half in range(2):
        for way in range(2):
            relay(0, way, half, z).start()
    def back_step(k, carry):
        step = lax.div(k + 1, 2)
        from_left = lax.rem(k, 2)
        h = lax.rem(z + NZ + (1 - 2 * from_left) * step, NZ)
        left = lax.rem(z + NZ - step, NZ)
        right = lax.rem(z + step, NZ)

        @pl.when(jnp.logical_and(from_left == 1, k < NZ - 3))
        def _():
            for half in range(2):
                relay(step - 1, 0, half, left).wait_recv()
                relay(step, 0, half, left).start()
                relay(step - 1, 1, half, right).wait_recv()
                relay(step, 1, half, right).start()

        @pl.when(k == NZ - 3)
        def _():
            relay(2, 0, 0, left).wait_recv()
            relay(3, 0, 0, left).start()
            relay(2, 1, 1, right).wait_recv()
            relay(3, 1, 1, right).start()
            relay(2, 0, 1, left).wait_recv()
            relay(2, 1, 0, right).wait_recv()

        @pl.when(k == NZ - 2)
        def _():
            for copy in by_copies:
                copy.wait_recv()
            big_stage[...] = ((big[:, y] + big_y[0]) + big_y[1]) + big_y[2]
            for copy in bz_copies:
                copy.start()

        @pl.when(k == NZ - 1)
        def _():
            relay(3, 0, 0, left).wait_recv()
            relay(3, 1, 1, left).wait_recv()

        row = pl.multiple_of(h * DH, DH)
        num_m[h, pl.ds(row, DH), :] = gbuf[h, 0:DH, :].astype(BF16)
        geo_m[h, pl.ds(row, DH), :] = gbuf[h, CUT:SUMS, :].astype(BF16)
        factor = sharp[h]
        field_token = gbuf[h, 0:DH, :].astype(BF16)
        geo_token = gbuf[h, CUT:SUMS, :].astype(BF16)
        for b in range(3):
            rows = slice(b * RB, (b + 1) * RB)
            token = num_m[h] if b == 0 else geo_m[h]
            grad_w = nn(feats[rows, :], token)
            if b == 0:
                grad_w = grad_w + nn(att_grad[...], mixm[h])
                grad_w = (grad_w + gbuf[h, DH : DH + 1, :]) * valid
            else:
                grad_w = grad_w + gbuf[h, DH + 1 : DH + 2, :]
            share = shares[h, rows, :]
            inside = jnp.sum(share * grad_w, axis=-1, keepdims=True)
            low = (share * (grad_w - inside) * factor).astype(BF16)
            slice_part[...] += nn(mid_t[pl.ds(row, DH), rows], low).reshape(NY, 8, M)
            acc_mid[pl.ds(row, DH), rows] = nt(w_slice[...], low).astype(BF16)
            acc_feat[pl.ds(row, DH), rows] = nt(
                field_token if b == 0 else geo_token, wlow[h, rows, :]
            ).astype(BF16)
        return carry

    lax.fori_loop(0, NZ, back_step, 0)
    feat_total = nt(normed_t[...], acc_feat[...])
    small[:, :, 0:8, :] = feat_total.reshape(NZ, NY, 8, D)
    mid_total = nt(normed_t[...], acc_mid[...])
    small[:, :, 8:16, :] = mid_total.reshape(NZ, NY, 8, D)
    ly_copies = [
        send(slice_part.at[lax.rem(y + k, NY)], slice_y.at[k - 1], sem_ly, k - 1, peer_y(z, y, k))
        for k in (2, 1, 3)
    ]
    sy_copies = [
        send(small.at[:, lax.rem(y + k, NY)], small_y.at[k - 1], sem_sy, k - 1, peer_y(z, y, k))
        for k in (2, 1, 3)
    ]
    for copy in ly_copies + sy_copies:
        copy.start()
    both = both_in[...]
    back_rows = wide(nn, both, d_scores[...])
    cross = wide(nt, both[:, 0:M], back_rows)
    mix_buf[z, :, 0:DH] = nn(cross, w_key[...], HIGH) * (1.0 / math.sqrt(DH))
    mix_buf[z, :, DH : 2 * DH] = tn(cross, w_query[...], HIGH) * (1.0 / math.sqrt(DH))
    mix_buf[z, :, 2 * DH : 3 * DH] = wide(nt, wide(nn, both, attn[...]), mg_sum[...])
    mix_buf[z, :, 3 * DH : 4 * DH] = jnp.zeros((DH, DH), F32)
    mix_copies = [
        send(mix_buf.at[z], mix_buf.at[z], sem_mix, k - 1, peer_z(z, y, k)) for k in ORDER
    ]
    for copy in ly_copies:
        copy.wait_recv()
    slice_z[0] = ((slice_part[y] + slice_y[0]) + slice_y[1]) + slice_y[2]
    lz_copies = [send(slice_z.at[0], slice_z.at[k], sem_lz, k - 1, peer_z(z, y, k)) for k in ORDER]
    for copy in lz_copies + mix_copies:
        copy.start()
    for copy in dz_copies:
        copy.wait_recv()
    total = down_stage[z]
    for k in range(NZ - 1):
        total = total + down_z[k]
    packed[0:DH] = total
    for copy in sy_copies:
        copy.wait_recv()
    small_stage[...] = ((small[:, y] + small_y[0]) + small_y[1]) + small_y[2]
    sz_copies = [
        send(small_stage.at[lax.rem(z + k, NZ)], small_z.at[k - 1], sem_sz, k - 1, peer_z(z, y, k))
        for k in ORDER
    ]
    for copy in sz_copies:
        copy.start()
    for copy in lz_copies:
        copy.wait_recv()
    slices = slice_z[z]
    for other in range(1, NZ):
        slices = slices + slice_z[lax.rem(z + NZ - other, NZ)]
    slice_all[y] = slices
    la_copies = [
        send(slice_all.at[y], slice_all.at[y], sem_la, k - 1, peer_y(z, y, k)) for k in (2, 1, 3)
    ]
    for copy in la_copies:
        copy.start()
    for copy in mix_copies:
        copy.wait_recv()
    mix = mix_buf[0]
    for h in range(1, HEADS):
        mix = mix + mix_buf[h]
    for i in range(3):
        mix_grad[i] = mix[:, i * DH : (i + 1) * DH]
    for copy in bz_copies:
        copy.wait_recv()
    total = big_stage[z]
    for k in range(NZ - 1):
        total = total + big_z[k]
    packed[DH : DH + BIG] = total
    for copy in la_copies:
        copy.wait_recv()
    packed[DH + BIG + SMALL : ROWS] = slice_all[...].reshape(DH, M)
    for copy in sz_copies:
        copy.wait_recv()
    total = small_stage[z]
    for k in range(NZ - 1):
        total = total + small_z[k]
    packed[DH + BIG : DH + BIG + SMALL] = total
    for copies in (
        z_copies,
        y_copies,
        m_copies,
        dy_copies,
        dz_copies,
        mz_copies,
        my_copies,
        by_copies,
        mix_copies,
        sy_copies,
        ly_copies,
        bz_copies,
        lz_copies,
        sz_copies,
        la_copies,
    ):
        for copy in copies:
            copy.wait_send()
    for step in range(4):
        for way in range(2):
            for half in range(2):
                if step < 3 or way == half:
                    relay(step, way, half, z).wait_send()


def result_kernel(
    layer_in,
    packed,
    mix_in,
    layer_out,
    feat_grad,
    mid_grad,
    out_grad,
    up_grad,
    down_grad,
    slice_grad,
    mix_grad,
):
    layer_out[...] = layer_in[...]
    down_grad[...] = packed[0:DH]
    for j in range(FF // D):
        up_grad[:, j * D : (j + 1) * D] = packed[DH + 8 * j : DH + 8 * j + 8]
    out_grad[...] = packed[2 * DH : 2 * DH + 8]
    feat_grad[...] = packed[2 * DH + 8 : 2 * DH + 16]
    mid_grad[...] = packed[2 * DH + 16 : 2 * DH + 24]
    slice_grad[...] = packed[2 * DH + 24 : ROWS]
    mix_grad[...] = mix_in[...]


def shape(dims, kind=F32):
    return jax.ShapeDtypeStruct(dims, kind)


def on_device(
    points,
    geometry,
    counts,
    cotangent,
    gain_attn,
    w_feat,
    w_mid,
    w_slice,
    sharpness,
    w_query,
    w_key,
    w_value,
    w_out,
    gain_mlp,
    w_up,
    w_down,
):
    vmem = pl.BlockSpec(memory_space=pltpu.VMEM)
    smem = pl.BlockSpec(memory_space=pltpu.SMEM)
    rows = 3 * RB

    def held(*dims):
        return pltpu.VMEM(dims, F32)

    def low(*dims):
        return pltpu.VMEM(dims, BF16)

    along_z = pltpu.SemaphoreType.DMA((2, NZ - 1))
    along_y = pltpu.SemaphoreType.DMA((2, NY - 1))
    layer, packed, mix = pl.pallas_call(
        layer_kernel,
        out_shape=(shape((RB, D), BF16), shape((ROWS, D)), shape((3, DH, DH))),
        in_specs=[vmem] * 3 + [smem] * 2 + [vmem] * 11,
        out_specs=(vmem,) * 3,
        scratch_shapes=[
            low(D, rows),
            low(rows, D),
            low(D, rows),
            low(rows, D),
            low(D, rows),
            held(HEADS, rows, M),
            low(HEADS, rows, M),
            low(HEADS, D, M),
            low(HEADS, D, M),
            low(HEADS, D, M),
            low(HEADS, D, M),
            held(RB, FF),
            low(RB, FF),
            low(RB, D),
            low(D, RB),
            low(RB, FF),
            low(RB, D),
            low(RB, D),
            low(RB, D),
            held(RB, D),
            low(D, rows),
            low(D, rows),
            held(DH, 2 * M),
            held(2 * M, M),
            held(2 * M, M),
            held(DH, M),
            held(HEADS, SUMS, M),
            held(NZ - 1, SUMS, M),
            held(NY, SUMS, M),
            held(HEADS, DH, M),
            held(HEADS, DH, M),
            held(NZ - 1, DH, M),
            held(NY, DH, M),
            held(HEADS, SUMS, M),
            held(HEADS, DH, 4 * DH),
            held(NZ, NY, DH, D),
            held(NY - 1, NZ, DH, D),
            held(NZ, DH, D),
            held(NZ - 1, DH, D),
            held(NZ, NY, BIG, D),
            held(NY - 1, NZ, BIG, D),
            held(NZ, BIG, D),
            held(NZ - 1, BIG, D),
            held(NZ, NY, SMALL, D),
            held(NY - 1, NZ, SMALL, D),
            held(NZ, SMALL, D),
            held(NZ - 1, SMALL, D),
            held(NY, 8, M),
            held(NY - 1, 8, M),
            held(NZ, 8, M),
            held(NY, 8, M),
            along_z,
            along_y,
            along_z,
            along_z,
            along_y,
            pltpu.SemaphoreType.DMA((2, 2, 2, 4)),
            along_z,
            along_y,
            along_z,
            along_y,
            along_z,
            along_y,
            along_z,
            along_y,
            along_z,
            along_y,
        ],
        compiler_params=pltpu.CompilerParams(
            collective_id=0, has_side_effects=True, vmem_limit_bytes=VMEM_BYTES
        ),
        name="layer",
    )(
        points,
        geometry,
        cotangent,
        counts,
        sharpness,
        gain_attn.reshape(1, D),
        gain_mlp.reshape(1, D),
        w_feat,
        w_mid,
        w_slice,
        w_query,
        w_key,
        w_value,
        w_out,
        w_up,
        w_down,
    )
    return pl.pallas_call(
        result_kernel,
        out_shape=(
            shape((RB, D), BF16),
            shape((8, D)),
            shape((8, D)),
            shape((8, D)),
            shape((8, FF)),
            shape((DH, D)),
            shape((DH, M)),
            shape((3, DH, DH)),
        ),
        in_specs=[vmem] * 3,
        out_specs=(vmem,) * 8,
        name="results",
    )(layer, packed, mix)


def solution(mesh):
    rows = P(("design", "pts"), None)
    return jax.shard_map(
        on_device,
        mesh=mesh,
        in_specs=(rows, rows, P(("design", "pts")), rows) + (P(),) * 12,
        out_specs=(rows,) * 6 + (P("design", None), P("design", None, None)),
        check_vma=False,
    )
```

```python
import math

import jax
import jax.numpy as jnp
from jax import lax
from jax.experimental import pallas as pl
from jax.experimental.pallas import tpu as pltpu
from jax.sharding import PartitionSpec as P

F32 = jnp.float32
BF16 = jnp.bfloat16
HIGH = lax.Precision.HIGHEST
NY = 4
NZ = 8
HEADS = 8
DH = 32
M = 256
D = 256
FF = 1024
RB = 256
SUMS = 72
BIG = 40
SMALL = 16
ROWS = 120
CUT = 40
EPS = 1e-05
VMEM_BYTES = 64000000
ORDER = (4, 3, 5, 2, 6, 1, 7)


def nn(a, b, precision=None):
    return lax.dot_general(
        a, b, (((1,), (0,)), ((), ())), precision=precision, preferred_element_type=F32
    )


def nt(a, b, precision=None):
    return lax.dot_general(
        a, b, (((1,), (1,)), ((), ())), precision=precision, preferred_element_type=F32
    )


def tn(a, b, precision=None):
    return lax.dot_general(
        a, b, (((0,), (0,)), ((), ())), precision=precision, preferred_element_type=F32
    )


def split(x):
    high = x.astype(BF16)
    return high, (x - high.astype(F32)).astype(BF16)


def wide(product, a, b):
    a_high, a_low = split(a)
    b_high, b_low = split(b)
    return product(a_high, b_high) + (product(a_low, b_high) + product(a_high, b_low))


def wide_tn(a, b):
    a_high, a_low = split(a)
    b_high, b_low = split(b)
    return tn(
        jnp.concatenate([a_high, a_low, a_high], axis=0),
        jnp.concatenate([b_high, b_high, b_low], axis=0),
    )


def norm_parts(x):
    centre = jnp.mean(x, axis=-1, keepdims=True)
    shifted = x - centre
    spread = jnp.mean(shifted * shifted, axis=-1, keepdims=True)
    scale = lax.rsqrt(spread + EPS)
    return shifted * scale, scale


def place():
    me = lax.axis_index("pts")
    return lax.div(me, NY), lax.rem(me, NY)


def peer_z(z, y, k):
    return {"pts": lax.rem(z + k, NZ) * NY + y}


def peer_y(z, y, k):
    return {"pts": z * NY + lax.rem(y + k, NY)}


def greet(z, y):
    barrier = pltpu.get_barrier_semaphore()
    for k in range(1, NZ):
        pl.semaphore_signal(barrier, inc=1, device_id=peer_z(z, y, k), device_id_type=pl.DeviceIdType.MESH)
    for k in range(1, NY):
        pl.semaphore_signal(barrier, inc=1, device_id=peer_y(z, y, k), device_id_type=pl.DeviceIdType.MESH)


def meet():
    pl.semaphore_wait(pltpu.get_barrier_semaphore(), NZ - 1 + NY - 1)


def send(src, dst, sems, device):
    return pltpu.make_async_remote_copy(
        src_ref=src,
        dst_ref=dst,
        send_sem=sems.at[0],
        recv_sem=sems.at[1],
        device_id=device,
        device_id_type=pl.DeviceIdType.MESH,
    )


def arrived(everything, sems):
    send(everything, everything, sems, {"pts": 0}).wait_recv()


def sent(everything, sems):
    send(everything, everything, sems, {"pts": 0}).wait_send()


def start(copies):
    for copy in copies:
        copy.start()


def swing(k):
    return 4 + (1 - 2 * lax.rem(k, 2)) * lax.div(k + 1, 2)


def layer_kernel(
    points,
    geometry,
    cotangent,
    counts,
    sharp,
    gain_attn,
    gain_mlp,
    w_feat,
    w_mid,
    w_slice,
    w_query,
    w_key,
    w_value,
    w_out,
    w_up,
    w_down,
    layer_out,
    packed,
    mix_grad,
    normed_t,
    feats,
    feat_t,
    mids,
    mid_t,
    shares,
    wlow,
    wsm,
    mixm,
    num_m,
    geo_m,
    grad_hid,
    low_hidden,
    low_up,
    low_up_t,
    grad_up_low,
    att_rows,
    res_rows,
    att_grad,
    res_hold,
    acc_feat,
    acc_mid,
    both_in,
    attn,
    d_scores,
    mg_sum,
    part_f,
    part_g,
    zbuf_f,
    zbuf_g,
    ybuf_f,
    ybuf_g,
    mbuf,
    mg_part,
    mg_z,
    mg_y,
    gbuf,
    mix_buf,
    down,
    down_y,
    down_stage,
    down_z,
    big,
    big_y,
    big_stage,
    big_z,
    small,
    small_y,
    small_stage,
    small_z,
    slice_part,
    slice_y,
    slice_z,
    slice_all,
    sem_g,
    sem_zf,
    sem_zg,
    sem_yf,
    sem_yg,
    sem_m,
    sem_mz,
    sem_my,
    sem_dy,
    sem_dz,
    sem_by,
    sem_bz,
    sem_sa,
    sem_sb,
    sem_sz,
    sem_ly,
    sem_lz,
    sem_la,
    sem_mix,
):
    z, y = place()
    greet(z, y)
    wsm[...] = jnp.zeros_like(wsm)
    for h in range(HEADS):
        wsm[h, h * DH : (h + 1) * DH, :] = w_slice[...]
    for b in range(3):
        rows = slice(b * RB, (b + 1) * RB)
        x = points[...] if b == 0 else geometry[(b - 1) * RB : b * RB, :]
        normed = norm_parts(x.astype(F32))[0] * gain_attn[...]
        normed_t[:, rows] = normed.T.astype(BF16)
        normed = normed.astype(BF16)
        found = nn(normed, w_feat[...])
        feats[rows, :] = found.astype(BF16)
        feat_t[:, rows] = found.T.astype(BF16)
        mids[rows, :] = nn(normed, w_mid[...]).astype(BF16)
    live = lax.broadcasted_iota(jnp.int32, (RB, 1), 0) < counts[0]
    valid = jnp.where(live, 1.0, 0.0).astype(F32)
    pick = lax.broadcasted_iota(jnp.int32, (8, M), 0)
    key_query = nt(w_key[...], w_query[...], HIGH) * (1.0 / math.sqrt(DH))
    meet()

    def shares_of(h, rows):
        logits = nn(mids[rows, :], wsm[h]) * sharp[h]
        powers = jnp.exp(logits - jnp.max(logits, axis=-1, keepdims=True))
        return powers * (1.0 / jnp.sum(powers, axis=-1, keepdims=True))

    def field_step(k, carry):
        h = lax.rem(z + swing(k), NZ)
        row = pl.multiple_of(h * DH, DH)
        rows = slice(0, RB)
        share = shares_of(h, rows)
        shares[h, rows, :] = share
        weights = share * valid
        low = weights.astype(BF16)
        wlow[h, rows, :] = low
        part_f[h] = nn(feat_t[pl.ds(row, DH), rows], low)
        part_g[h, DH:CUT, :] = jnp.where(pick == 0, jnp.sum(weights, axis=0, keepdims=True), 0.0)

        @pl.when(k < NZ - 1)
        def _():
            send(part_f.at[h], zbuf_f.at[k], sem_zf, peer_z(z, y, swing(k))).start()

        return carry

    def geo_step(k, carry):
        h = lax.rem(z + swing(k), NZ)
        row = pl.multiple_of(h * DH, DH)
        numers = []
        denoms = []
        for b in range(1, 3):
            rows = slice(b * RB, (b + 1) * RB)
            share = shares_of(h, rows)
            shares[h, rows, :] = share
            low = share.astype(BF16)
            wlow[h, rows, :] = low
            denoms.append(jnp.sum(share, axis=0, keepdims=True))
            numers.append(nn(feat_t[pl.ds(row, DH), rows], low))
        part_g[h, 0:DH, :] = numers[0] + numers[1]
        part_g[h, DH:CUT, :] = jnp.where(pick == 1, denoms[0] + denoms[1], part_g[h, DH:CUT, :])

        @pl.when(k < NZ - 1)
        def _():
            send(part_g.at[h], zbuf_g.at[k], sem_zg, peer_z(z, y, swing(k))).start()

        return carry

    lax.fori_loop(0, NZ, field_step, 0)
    lax.fori_loop(0, NZ, geo_step, 0)
    arrived(zbuf_f, sem_zf)
    total = part_f[z]
    for i in range(NZ - 1):
        total = total + zbuf_f[i]
    ybuf_f[0] = total
    start([send(ybuf_f.at[0], ybuf_f.at[k], sem_yf, peer_y(z, y, k)) for k in (2, 1, 3)])
    for b in range(3):
        rows = slice(b * RB, (b + 1) * RB)
        mid_t[:, rows] = mids[rows, :].astype(F32).T.astype(BF16)
    mixm[...] = jnp.zeros_like(mixm)
    num_m[...] = jnp.zeros_like(num_m)
    geo_m[...] = jnp.zeros_like(geo_m)
    slice_part[...] = jnp.zeros_like(slice_part)
    arrived(zbuf_g, sem_zg)
    total = part_g[z]
    for i in range(NZ - 1):
        total = total + zbuf_g[i]
    ybuf_g[0] = total
    start([send(ybuf_g.at[0], ybuf_g.at[k], sem_yg, peer_y(z, y, k)) for k in (2, 1, 3)])
    arrived(ybuf_f.at[1:NY], sem_yf)
    sums = ybuf_f[y]
    for other in range(1, NY):
        sums = sums + ybuf_f[lax.rem(y + NY - other, NY)]
    arrived(ybuf_g.at[1:NY], sem_yg)
    geo_sums = ybuf_g[y]
    for other in range(1, NY):
        geo_sums = geo_sums + ybuf_g[lax.rem(y + NY - other, NY)]
    den = geo_sums[DH : DH + 1] + EPS
    geo_den = geo_sums[DH + 1 : DH + 2] + EPS
    field = sums / den
    both = jnp.concatenate([field, geo_sums[0:DH] / geo_den], axis=1)
    both_in[...] = both
    query = wide(nn, key_query, field)
    values = wide(tn, w_value[...], both)
    scores = wide_tn(both, query)
    powers = jnp.exp(scores - jnp.max(scores, axis=0, keepdims=True))
    attention = powers * (1.0 / jnp.sum(powers, axis=0, keepdims=True))
    attn[...] = attention
    mbuf[z] = wide(nn, values, attention)
    m_copies = [send(mbuf.at[z], mbuf.at[z], sem_m, peer_z(z, y, k)) for k in ORDER]
    start(m_copies)
    for j in range(FF // D):
        cols = slice(j * D, (j + 1) * D)
        grad_hid[:, cols] = nt(cotangent[...], w_down[cols, :])
    key_side = wide(tn, key_query, both)
    arrived(mbuf.at[1:NZ], sem_m)
    for h in range(HEADS):
        mixm[h, h * DH : (h + 1) * DH, :] = mbuf[h].astype(BF16)
    attended = nt(wlow[0, 0:RB, :], mixm[0])
    for h in range(1, HEADS):
        attended = attended + nt(wlow[h, 0:RB, :], mixm[h])
    attended = attended.astype(BF16)
    att_rows[...] = attended
    residual = points[...].astype(F32) + nn(attended, w_out[...])
    hat, scale = norm_parts(residual)
    second_low = (hat * gain_mlp[...]).astype(BF16)
    low_up[...] = second_low
    const = math.sqrt(2.0 / math.pi)
    res_hold[...] = residual
    grad_second = jnp.zeros((RB, D), F32)
    for j in range(FF // D):
        cols = slice(j * D, (j + 1) * D)
        upper = nn(second_low, w_up[:, cols])
        square = upper * upper
        half = 0.5 + 0.5 * jnp.tanh(upper * (const + (0.044715 * const) * square))
        hidden = upper * half
        down[2 * j : 2 * j + 2] = nn(hidden.T.astype(BF16), cotangent[...]).reshape(2, NY, DH, D)
        low_hidden[:, cols] = hidden.astype(BF16)
        steep = upper * (2.0 * const + (6.0 * 0.044715 * const) * square)
        slope = half * (1.0 + steep * (1.0 - half))
        grad_upper = (grad_hid[:, cols] * slope).astype(BF16)
        grad_up_low[:, cols] = grad_upper
        grad_second = grad_second + nt(grad_upper, w_up[:, cols])
    dy_copies = [
        send(down.at[:, lax.rem(y + k, NY)], down_y.at[k - 1], sem_dy, peer_y(z, y, k))
        for k in (2, 1, 3)
    ]
    start(dy_copies)
    scaled = grad_second * gain_mlp[...]
    back = scale * (
        scaled
        - jnp.mean(scaled, axis=-1, keepdims=True)
        - hat * jnp.mean(scaled * hat, axis=-1, keepdims=True)
    )
    grad_resid = (cotangent[...].astype(F32) + back).astype(BF16)
    res_rows[...] = grad_resid
    grad_att = nt(grad_resid, w_out[...])
    att_grad[...] = grad_att.astype(BF16)
    att_t = grad_att.T.astype(BF16)
    for h in range(HEADS):
        mg_part[h] = nn(att_t[h * DH : (h + 1) * DH, :], wlow[h, 0:RB, :])
    mz_copies = [
        send(mg_part.at[lax.rem(z + k, NZ)], mg_z.at[k - 1], sem_mz, peer_z(z, y, k))
        for k in ORDER
    ]
    start(mz_copies)
    low_up_t[...] = low_up[...].astype(F32).T.astype(BF16)

    def grads_step(j, carry):
        cols = pl.ds(pl.multiple_of(j * D, D), D)
        up = nn(low_up_t[...], grad_up_low[:, cols])
        big[:, :, pl.ds(pl.multiple_of(8 * j, 8), 8), :] = up.reshape(NZ, NY, 8, D)
        res_hold[...] += nn(low_hidden[:, cols], w_down[cols, :])
        return carry

    lax.fori_loop(0, FF // D, grads_step, 0)
    layer_out[...] = res_hold[...].astype(BF16)
    out = nn(att_rows[...].astype(F32).T.astype(BF16), res_rows[...])
    big[:, :, DH:BIG, :] = out.reshape(NZ, NY, 8, D)
    arrived(mg_z, sem_mz)
    total = mg_part[z]
    for k in range(NZ - 1):
        total = total + mg_z[k]
    mg_y[0] = total
    my_copies = [
        send(mg_y.at[0], mg_y.at[k], sem_my, peer_y(z, y, k)) for k in (2, 1, 3)
    ]
    start(my_copies)
    by_copies = [
        send(big.at[:, lax.rem(y + k, NY)], big_y.at[k - 1], sem_by, peer_y(z, y, k))
        for k in (2, 1, 3)
    ]
    start(by_copies)
    bz_copies = [
        send(big_stage.at[lax.rem(z + k, NZ)], big_z.at[k - 1], sem_bz, peer_z(z, y, k))
        for k in ORDER
    ]
    arrived(down_y, sem_dy)
    down_stage[...] = ((down[:, y] + down_y[0]) + down_y[1]) + down_y[2]
    dz_copies = [
        send(down_stage.at[lax.rem(z + k, NZ)], down_z.at[k - 1], sem_dz, peer_z(z, y, k))
        for k in ORDER
    ]
    start(dz_copies)
    arrived(mg_y.at[1:NY], sem_my)
    grad = mg_y[y]
    for other in range(1, NY):
        grad = grad + mg_y[lax.rem(y + NY - other, NY)]
    mg_sum[...] = grad
    value_side = wide(nn, w_value[...], grad)
    d_attn = wide_tn(both, value_side)
    inner = jnp.sum(attention * d_attn, axis=0, keepdims=True)
    d_score = attention * (d_attn - inner)
    d_scores[...] = d_score
    d_both = wide(nt, query, d_score) + wide(nt, value_side, attention)
    d_field = (d_both[:, 0:M] + wide(nn, key_side, d_score)) / den
    d_geo = d_both[:, M : 2 * M] / geo_den
    den_grad = -jnp.sum(d_field * both[:, 0:M], axis=0, keepdims=True)
    geo_den_grad = -jnp.sum(d_geo * both[:, M : 2 * M], axis=0, keepdims=True)
    gbuf[z, 0:DH, :] = d_field
    gbuf[z, DH:CUT, :] = jnp.where(pick == 0, den_grad, jnp.where(pick == 1, geo_den_grad, 0.0))
    gbuf[z, CUT:SUMS, :] = d_geo

    def relay(step, way, half, origin):
        piece = gbuf.at[origin, half * CUT : CUT + half * DH]
        return pltpu.make_async_remote_copy(
            src_ref=piece,
            dst_ref=piece,
            send_sem=sem_g.at[0, way, half, step],
            recv_sem=sem_g.at[1, way, half, step],
            device_id=peer_z(z, y, 1 if way == 0 else NZ - 1),
            device_id_type=pl.DeviceIdType.MESH,
        )

    for half in range(2):
        for way in range(2):
            relay(0, way, half, z).start()
    def back_step(k, carry):
        step = lax.div(k + 1, 2)
        from_left = lax.rem(k, 2)
        h = lax.rem(z + NZ + (1 - 2 * from_left) * step, NZ)
        left = lax.rem(z + NZ - step, NZ)
        right = lax.rem(z + step, NZ)

        @pl.when(jnp.logical_and(from_left == 1, k < NZ - 3))
        def _():
            for half in range(2):
                relay(step - 1, 0, half, left).wait_recv()
                relay(step, 0, half, left).start()
                relay(step - 1, 1, half, right).wait_recv()
                relay(step, 1, half, right).start()

        @pl.when(k == NZ - 3)
        def _():
            relay(2, 0, 0, left).wait_recv()
            relay(3, 0, 0, left).start()
            relay(2, 1, 1, right).wait_recv()
            relay(3, 1, 1, right).start()
            relay(2, 0, 1, left).wait_recv()
            relay(2, 1, 0, right).wait_recv()

        @pl.when(k == NZ - 1)
        def _():
            relay(3, 0, 0, left).wait_recv()
            relay(3, 1, 1, left).wait_recv()

        row = pl.multiple_of(h * DH, DH)
        spot = pl.multiple_of(lax.rem(h - z + NZ + 2, NZ) * DH, DH)
        num_m[h, pl.ds(row, DH), :] = gbuf[h, 0:DH, :].astype(BF16)
        geo_m[h, pl.ds(row, DH), :] = gbuf[h, CUT:SUMS, :].astype(BF16)
        factor = sharp[h]
        field_token = gbuf[h, 0:DH, :].astype(BF16)
        geo_token = gbuf[h, CUT:SUMS, :].astype(BF16)
        for b in range(3):
            rows = slice(b * RB, (b + 1) * RB)
            token = num_m[h] if b == 0 else geo_m[h]
            grad_w = nn(feats[rows, :], token)
            if b == 0:
                grad_w = grad_w + nn(att_grad[...], mixm[h])
                grad_w = (grad_w + gbuf[h, DH : DH + 1, :]) * valid
            else:
                grad_w = grad_w + gbuf[h, DH + 1 : DH + 2, :]
            share = shares[h, rows, :]
            inside = jnp.sum(share * grad_w, axis=-1, keepdims=True)
            low = (share * (grad_w - inside) * factor).astype(BF16)
            slice_part[...] += nn(mid_t[pl.ds(row, DH), rows], low).reshape(NY, 8, M)
            acc_mid[pl.ds(spot, DH), rows] = nt(w_slice[...], low).astype(BF16)
            acc_feat[pl.ds(spot, DH), rows] = nt(
                field_token if b == 0 else geo_token, wlow[h, rows, :]
            ).astype(BF16)
        return carry

    def narrow(which, rows):
        feat_half = nt(normed_t[...], acc_feat[rows, :])
        small[which, :, :, 0:8, :] = feat_half.reshape(NZ, NY, 8, D // 2)
        mid_half = nt(normed_t[...], acc_mid[rows, :])
        small[which, :, :, 8:SMALL, :] = mid_half.reshape(NZ, NY, 8, D // 2)
        start(
            [
                send(
                    small.at[which, :, lax.rem(y + k, NY)],
                    small_y.at[which, k - 1],
                    sem_sa if which == 0 else sem_sb,
                    peer_y(z, y, k),
                )
                for k in (2, 1, 3)
            ]
        )

    lax.fori_loop(0, HEADS // 2, back_step, 0)
    narrow(0, slice(0, D // 2))
    lax.fori_loop(HEADS // 2, HEADS, back_step, 0)
    start(
        [
            send(slice_part.at[lax.rem(y + k, NY)], slice_y.at[k - 1], sem_ly, peer_y(z, y, k))
            for k in (2, 1, 3)
        ]
    )
    narrow(1, slice(D // 2, D))
    arrived(big_y, sem_by)
    big_stage[...] = ((big[:, y] + big_y[0]) + big_y[1]) + big_y[2]
    start(bz_copies)
    both = both_in[...]
    back_rows = wide(nn, both, d_scores[...])
    cross = wide(nt, both[:, 0:M], back_rows)
    mix_buf[z, :, 0:DH] = nn(cross, w_key[...], HIGH) * (1.0 / math.sqrt(DH))
    mix_buf[z, :, DH : 2 * DH] = tn(cross, w_query[...], HIGH) * (1.0 / math.sqrt(DH))
    mix_buf[z, :, 2 * DH : 3 * DH] = wide(nt, wide(nn, both, attn[...]), mg_sum[...])
    mix_buf[z, :, 3 * DH : 4 * DH] = jnp.zeros((DH, DH), F32)
    mix_copies = [
        send(mix_buf.at[z], mix_buf.at[z], sem_mix, peer_z(z, y, k)) for k in ORDER
    ]
    arrived(slice_y, sem_ly)
    slice_z[0] = ((slice_part[y] + slice_y[0]) + slice_y[1]) + slice_y[2]
    lz_copies = [send(slice_z.at[0], slice_z.at[k], sem_lz, peer_z(z, y, k)) for k in ORDER]
    start(lz_copies + mix_copies)
    arrived(down_z, sem_dz)
    total = down_stage[z]
    for k in range(NZ - 1):
        total = total + down_z[k]
    packed[0:DH] = total
    halves = []
    for which in range(2):
        arrived(small_y.at[which], sem_sa if which == 0 else sem_sb)
        halves.append(
            ((small[which, :, y] + small_y[which, 0]) + small_y[which, 1]) + small_y[which, 2]
        )
    turned = jnp.concatenate(halves, axis=2).reshape(NZ * SMALL, D)
    turned = pltpu.roll(turned, lax.rem(z + NZ - 2, NZ) * DH, 1)
    small_stage[...] = turned.reshape(NZ, SMALL, D)
    sz_copies = [
        send(small_stage.at[lax.rem(z + k, NZ)], small_z.at[k - 1], sem_sz, peer_z(z, y, k))
        for k in ORDER
    ]
    start(sz_copies)
    arrived(slice_z.at[1:NZ], sem_lz)
    slices = slice_z[z]
    for other in range(1, NZ):
        slices = slices + slice_z[lax.rem(z + NZ - other, NZ)]
    slice_all[y] = slices
    la_copies = [
        send(slice_all.at[y], slice_all.at[y], sem_la, peer_y(z, y, k)) for k in (2, 1, 3)
    ]
    start(la_copies)
    arrived(mix_buf.at[1:NZ], sem_mix)
    mix = mix_buf[0]
    for h in range(1, HEADS):
        mix = mix + mix_buf[h]
    for i in range(3):
        mix_grad[i] = mix[:, i * DH : (i + 1) * DH]
    arrived(big_z, sem_bz)
    total = big_stage[z]
    for k in range(NZ - 1):
        total = total + big_z[k]
    packed[DH : DH + BIG] = total
    arrived(slice_all.at[1:NY], sem_la)
    packed[DH + BIG + SMALL : ROWS] = slice_all[...].reshape(DH, M)
    arrived(small_z, sem_sz)
    total = small_stage[z]
    for k in range(NZ - 1):
        total = total + small_z[k]
    packed[DH + BIG : DH + BIG + SMALL] = total
    for everything, sems in (
        (zbuf_f, sem_zf),
        (zbuf_g, sem_zg),
        (ybuf_f.at[1:NY], sem_yf),
        (ybuf_g.at[1:NY], sem_yg),
        (mbuf.at[1:NZ], sem_m),
        (mg_z, sem_mz),
        (mg_y.at[1:NY], sem_my),
        (down_y, sem_dy),
        (down_z, sem_dz),
        (big_y, sem_by),
        (big_z, sem_bz),
        (small_y.at[0], sem_sa),
        (small_y.at[1], sem_sb),
        (small_z, sem_sz),
        (slice_y, sem_ly),
        (slice_z.at[1:NZ], sem_lz),
        (slice_all.at[1:NY], sem_la),
        (mix_buf.at[1:NZ], sem_mix),
    ):
        sent(everything, sems)
    for step in range(4):
        for way in range(2):
            for half in range(2):
                if step < 3 or way == half:
                    relay(step, way, half, z).wait_send()


def result_kernel(
    layer_in,
    packed,
    mix_in,
    layer_out,
    feat_grad,
    mid_grad,
    out_grad,
    up_grad,
    down_grad,
    slice_grad,
    mix_grad,
):
    layer_out[...] = layer_in[...]
    down_grad[...] = packed[0:DH]
    for j in range(FF // D):
        up_grad[:, j * D : (j + 1) * D] = packed[DH + 8 * j : DH + 8 * j + 8]
    out_grad[...] = packed[2 * DH : 2 * DH + 8]
    feat_grad[...] = packed[2 * DH + 8 : 2 * DH + 16]
    mid_grad[...] = packed[2 * DH + 16 : 2 * DH + 24]
    slice_grad[...] = packed[2 * DH + 24 : ROWS]
    mix_grad[...] = mix_in[...]


def shape(dims, kind=F32):
    return jax.ShapeDtypeStruct(dims, kind)


def on_device(
    points,
    geometry,
    counts,
    cotangent,
    gain_attn,
    w_feat,
    w_mid,
    w_slice,
    sharpness,
    w_query,
    w_key,
    w_value,
    w_out,
    gain_mlp,
    w_up,
    w_down,
):
    vmem = pl.BlockSpec(memory_space=pltpu.VMEM)
    smem = pl.BlockSpec(memory_space=pltpu.SMEM)
    rows = 3 * RB

    def held(*dims):
        return pltpu.VMEM(dims, F32)

    def low(*dims):
        return pltpu.VMEM(dims, BF16)

    layer, packed, mix = pl.pallas_call(
        layer_kernel,
        out_shape=(shape((RB, D), BF16), shape((ROWS, D)), shape((3, DH, DH))),
        in_specs=[vmem] * 3 + [smem] * 2 + [vmem] * 11,
        out_specs=(vmem,) * 3,
        scratch_shapes=[
            low(D, rows),
            low(rows, D),
            low(D, rows),
            low(rows, D),
            low(D, rows),
            held(HEADS, rows, M),
            low(HEADS, rows, M),
            low(HEADS, D, M),
            low(HEADS, D, M),
            low(HEADS, D, M),
            low(HEADS, D, M),
            held(RB, FF),
            low(RB, FF),
            low(RB, D),
            low(D, RB),
            low(RB, FF),
            low(RB, D),
            low(RB, D),
            low(RB, D),
            held(RB, D),
            low(D, rows),
            low(D, rows),
            held(DH, 2 * M),
            held(2 * M, M),
            held(2 * M, M),
            held(DH, M),
            held(HEADS, DH, M),
            held(HEADS, CUT, M),
            held(NZ - 1, DH, M),
            held(NZ - 1, CUT, M),
            held(NY, DH, M),
            held(NY, CUT, M),
            held(HEADS, DH, M),
            held(HEADS, DH, M),
            held(NZ - 1, DH, M),
            held(NY, DH, M),
            held(HEADS, SUMS, M),
            held(HEADS, DH, 4 * DH),
            held(NZ, NY, DH, D),
            held(NY - 1, NZ, DH, D),
            held(NZ, DH, D),
            held(NZ - 1, DH, D),
            held(NZ, NY, BIG, D),
            held(NY - 1, NZ, BIG, D),
            held(NZ, BIG, D),
            held(NZ - 1, BIG, D),
            held(2, NZ, NY, SMALL, D // 2),
            held(2, NY - 1, NZ, SMALL, D // 2),
            held(NZ, SMALL, D),
            held(NZ - 1, SMALL, D),
            held(NY, 8, M),
            held(NY - 1, 8, M),
            held(NZ, 8, M),
            held(NY, 8, M),
            pltpu.SemaphoreType.DMA((2, 2, 2, 4)),
        ]
        + [pltpu.SemaphoreType.DMA((2,))] * 18,
        compiler_params=pltpu.CompilerParams(
            collective_id=0, has_side_effects=True, vmem_limit_bytes=VMEM_BYTES
        ),
        name="layer",
    )(
        points,
        geometry,
        cotangent,
        counts,
        sharpness,
        gain_attn.reshape(1, D),
        gain_mlp.reshape(1, D),
        w_feat,
        w_mid,
        w_slice,
        w_query,
        w_key,
        w_value,
        w_out,
        w_up,
        w_down,
    )
    return pl.pallas_call(
        result_kernel,
        out_shape=(
            shape((RB, D), BF16),
            shape((8, D)),
            shape((8, D)),
            shape((8, D)),
            shape((8, FF)),
            shape((DH, D)),
            shape((DH, M)),
            shape((3, DH, DH)),
        ),
        in_specs=[vmem] * 3,
        out_specs=(vmem,) * 8,
        name="results",
    )(layer, packed, mix)


def solution(mesh):
    rows = P(("design", "pts"), None)
    return jax.shard_map(
        on_device,
        mesh=mesh,
        in_specs=(rows, rows, P(("design", "pts")), rows) + (P(),) * 12,
        out_specs=(rows,) * 6 + (P("design", None), P("design", None, None)),
        check_vma=False,
    )
```

```python
import math

import jax
import jax.numpy as jnp
from jax import lax
from jax.experimental import pallas as pl
from jax.experimental.pallas import tpu as pltpu
from jax.sharding import PartitionSpec as P

F32 = jnp.float32
BF16 = jnp.bfloat16
HIGH = lax.Precision.HIGHEST
NY = 4
NZ = 8
HEADS = 8
DH = 32
M = 256
D = 256
FF = 1024
RB = 256
SUMS = 72
BIG = 24
EARLY = 24
SMALL = 16
ROWS = 120
CUT = 40
STRIP = 128
EPS = 1e-05
VMEM_BYTES = 64000000
ORDER = (4, 3, 5, 2, 6, 1, 7)


def nn(a, b, precision=None):
    return lax.dot_general(
        a, b, (((1,), (0,)), ((), ())), precision=precision, preferred_element_type=F32
    )


def nt(a, b, precision=None):
    return lax.dot_general(
        a, b, (((1,), (1,)), ((), ())), precision=precision, preferred_element_type=F32
    )


def tn(a, b, precision=None):
    return lax.dot_general(
        a, b, (((0,), (0,)), ((), ())), precision=precision, preferred_element_type=F32
    )


def split(x):
    high = x.astype(BF16)
    return high, (x - high.astype(F32)).astype(BF16)


def wide(product, a, b):
    a_high, a_low = split(a)
    b_high, b_low = split(b)
    return product(a_high, b_high) + (product(a_low, b_high) + product(a_high, b_low))


def wide_tn(a, b):
    a_high, a_low = split(a)
    b_high, b_low = split(b)
    return tn(
        jnp.concatenate([a_high, a_low, a_high], axis=0),
        jnp.concatenate([b_high, b_high, b_low], axis=0),
    )


def norm_parts(x):
    centre = jnp.mean(x, axis=-1, keepdims=True)
    shifted = x - centre
    spread = jnp.mean(shifted * shifted, axis=-1, keepdims=True)
    scale = lax.rsqrt(spread + EPS)
    return shifted * scale, scale


def place():
    me = lax.axis_index("pts")
    return lax.div(me, NY), lax.rem(me, NY)


def peer_z(z, y, k):
    return {"pts": lax.rem(z + k, NZ) * NY + y}


def peer_y(z, y, k):
    return {"pts": z * NY + lax.rem(y + k, NY)}


def greet(z, y):
    barrier = pltpu.get_barrier_semaphore()
    for k in range(1, NZ):
        pl.semaphore_signal(barrier, inc=1, device_id=peer_z(z, y, k), device_id_type=pl.DeviceIdType.MESH)
    for k in range(1, NY):
        pl.semaphore_signal(barrier, inc=1, device_id=peer_y(z, y, k), device_id_type=pl.DeviceIdType.MESH)


def meet():
    pl.semaphore_wait(pltpu.get_barrier_semaphore(), NZ - 1 + NY - 1)


def send(src, dst, sems, device):
    return pltpu.make_async_remote_copy(
        src_ref=src,
        dst_ref=dst,
        send_sem=sems.at[0],
        recv_sem=sems.at[1],
        device_id=device,
        device_id_type=pl.DeviceIdType.MESH,
    )


def arrived(everything, sems):
    send(everything, everything, sems, {"pts": 0}).wait_recv()


def sent(everything, sems):
    send(everything, everything, sems, {"pts": 0}).wait_send()


def start(copies):
    for copy in copies:
        copy.start()


def swing(k):
    return 4 + (1 - 2 * lax.rem(k, 2)) * lax.div(k + 1, 2)


def layer_kernel(
    points,
    geometry,
    cotangent,
    counts,
    sharp,
    gain_attn,
    gain_mlp,
    w_feat,
    w_mid,
    w_slice,
    w_query,
    w_key,
    w_value,
    w_out,
    w_up,
    w_down,
    layer_out,
    packed,
    mix_grad,
    normed_t,
    feats,
    feat_t,
    mids,
    mid_t,
    shares,
    wlow,
    wsm,
    mixm,
    num_m,
    geo_m,
    grad_hid,
    low_hidden,
    low_up,
    low_up_t,
    grad_up_low,
    att_rows,
    res_rows,
    att_grad,
    res_hold,
    acc_feat,
    acc_mid,
    both_in,
    attn,
    d_scores,
    mg_sum,
    part_f,
    part_g,
    zbuf_f,
    zbuf_g,
    ybuf_f,
    ybuf_g,
    mbuf,
    mg_part,
    mg_z,
    mg_y,
    gbuf,
    mix_part,
    down,
    down_y,
    down_stage,
    down_z,
    big,
    big_y,
    big_stage,
    big_z,
    small,
    small_y,
    small_stage,
    small_z,
    slice_part,
    slice_y,
    slice_z,
    slice_all,
    sem_g,
    sem_by,
    sem_bz,
    sem_zf,
    sem_zg,
    sem_yf,
    sem_yg,
    sem_m,
    sem_mz,
    sem_my,
    sem_dy,
    sem_dz,
    sem_sa,
    sem_sb,
    sem_sz,
    sem_ly,
    sem_lz,
    sem_la,
):
    z, y = place()
    greet(z, y)
    wsm[...] = jnp.zeros_like(wsm)
    for h in range(HEADS):
        wsm[h, h * DH : (h + 1) * DH, :] = w_slice[...]
    for b in range(3):
        rows = slice(b * RB, (b + 1) * RB)
        x = points[...] if b == 0 else geometry[(b - 1) * RB : b * RB, :]
        normed = norm_parts(x.astype(F32))[0] * gain_attn[...]
        normed_t[:, rows] = normed.T.astype(BF16)
        normed = normed.astype(BF16)
        found = nn(normed, w_feat[...])
        feats[rows, :] = found.astype(BF16)
        feat_t[:, rows] = found.T.astype(BF16)
        mids[rows, :] = nn(normed, w_mid[...]).astype(BF16)
    live = lax.broadcasted_iota(jnp.int32, (RB, 1), 0) < counts[0]
    valid = jnp.where(live, 1.0, 0.0).astype(F32)
    pick = lax.broadcasted_iota(jnp.int32, (8, M), 0)
    key_query = nt(w_key[...], w_query[...], HIGH) * (1.0 / math.sqrt(DH))
    meet()

    def shares_of(h, rows):
        logits = nn(mids[rows, :], wsm[h]) * sharp[h]
        powers = jnp.exp(logits - jnp.max(logits, axis=-1, keepdims=True))
        return powers * (1.0 / jnp.sum(powers, axis=-1, keepdims=True))

    def field_step(k, carry):
        h = lax.rem(z + swing(k), NZ)
        row = pl.multiple_of(h * DH, DH)
        rows = slice(0, RB)
        share = shares_of(h, rows)
        shares[h, rows, :] = share
        weights = share * valid
        low = weights.astype(BF16)
        wlow[h, rows, :] = low
        part_f[h] = nn(feat_t[pl.ds(row, DH), rows], low)
        part_g[h, DH:CUT, :] = jnp.where(pick == 0, jnp.sum(weights, axis=0, keepdims=True), 0.0)

        @pl.when(k < NZ - 1)
        def _():
            send(part_f.at[h], zbuf_f.at[k], sem_zf, peer_z(z, y, swing(k))).start()

        return carry

    def geo_step(k, carry):
        h = lax.rem(z + swing(k), NZ)
        row = pl.multiple_of(h * DH, DH)
        numers = []
        denoms = []
        for b in range(1, 3):
            rows = slice(b * RB, (b + 1) * RB)
            share = shares_of(h, rows)
            shares[h, rows, :] = share
            low = share.astype(BF16)
            wlow[h, rows, :] = low
            denoms.append(jnp.sum(share, axis=0, keepdims=True))
            numers.append(nn(feat_t[pl.ds(row, DH), rows], low))
        part_g[h, 0:DH, :] = numers[0] + numers[1]
        part_g[h, DH:CUT, :] = jnp.where(pick == 1, denoms[0] + denoms[1], part_g[h, DH:CUT, :])

        @pl.when(k < NZ - 1)
        def _():
            send(part_g.at[h], zbuf_g.at[k], sem_zg, peer_z(z, y, swing(k))).start()

        return carry

    lax.fori_loop(0, NZ, field_step, 0)
    lax.fori_loop(0, NZ, geo_step, 0)
    arrived(zbuf_f, sem_zf)
    total = part_f[z]
    for i in range(NZ - 1):
        total = total + zbuf_f[i]
    ybuf_f[0] = total
    start([send(ybuf_f.at[0], ybuf_f.at[k], sem_yf, peer_y(z, y, k)) for k in (2, 1, 3)])
    for b in range(3):
        rows = slice(b * RB, (b + 1) * RB)
        mid_t[:, rows] = mids[rows, :].astype(F32).T.astype(BF16)
    mixm[...] = jnp.zeros_like(mixm)
    num_m[...] = jnp.zeros_like(num_m)
    geo_m[...] = jnp.zeros_like(geo_m)
    slice_part[...] = jnp.zeros_like(slice_part)
    arrived(zbuf_g, sem_zg)
    total = part_g[z]
    for i in range(NZ - 1):
        total = total + zbuf_g[i]
    ybuf_g[0] = total
    start([send(ybuf_g.at[0], ybuf_g.at[k], sem_yg, peer_y(z, y, k)) for k in (2, 1, 3)])
    arrived(ybuf_f.at[1:NY], sem_yf)
    sums = ybuf_f[y]
    for other in range(1, NY):
        sums = sums + ybuf_f[lax.rem(y + NY - other, NY)]
    arrived(ybuf_g.at[1:NY], sem_yg)
    geo_sums = ybuf_g[y]
    for other in range(1, NY):
        geo_sums = geo_sums + ybuf_g[lax.rem(y + NY - other, NY)]
    den = geo_sums[DH : DH + 1] + EPS
    geo_den = geo_sums[DH + 1 : DH + 2] + EPS
    field = sums / den
    both = jnp.concatenate([field, geo_sums[0:DH] / geo_den], axis=1)
    both_in[...] = both
    query = wide(nn, key_query, field)
    values = wide(tn, w_value[...], both)
    scores = wide_tn(both, query)
    powers = jnp.exp(scores - jnp.max(scores, axis=0, keepdims=True))
    attention = powers * (1.0 / jnp.sum(powers, axis=0, keepdims=True))
    attn[...] = attention
    mbuf[z] = wide(nn, values, attention)
    m_copies = [send(mbuf.at[z], mbuf.at[z], sem_m, peer_z(z, y, k)) for k in ORDER]
    start(m_copies)
    for j in range(FF // D):
        cols = slice(j * D, (j + 1) * D)
        grad_hid[:, cols] = nt(cotangent[...], w_down[cols, :])
    key_side = wide(tn, key_query, both)
    arrived(mbuf.at[1:NZ], sem_m)
    for h in range(HEADS):
        mixm[h, h * DH : (h + 1) * DH, :] = mbuf[h].astype(BF16)
    attended = nt(wlow[0, 0:RB, :], mixm[0])
    for h in range(1, HEADS):
        attended = attended + nt(wlow[h, 0:RB, :], mixm[h])
    attended = attended.astype(BF16)
    att_rows[...] = attended
    residual = points[...].astype(F32) + nn(attended, w_out[...])
    hat, scale = norm_parts(residual)
    second_low = (hat * gain_mlp[...]).astype(BF16)
    low_up[...] = second_low
    const = math.sqrt(2.0 / math.pi)
    res_hold[...] = residual
    grad_second = jnp.zeros((RB, D), F32)
    for j in range(FF // D):
        cols = slice(j * D, (j + 1) * D)
        for r in range(RB // STRIP):
            strip = slice(r * STRIP, (r + 1) * STRIP)
            upper = nn(low_up[strip, :], w_up[:, cols])
            square = upper * upper
            half = 0.5 + 0.5 * jnp.tanh(upper * (const + (0.044715 * const) * square))
            hidden = upper * half
            low_hidden[strip, cols] = hidden.astype(BF16)
            steep = upper * (2.0 * const + (6.0 * 0.044715 * const) * square)
            slope = half * (1.0 + steep * (1.0 - half))
            grad_up_low[strip, cols] = (grad_hid[strip, cols] * slope).astype(BF16)
        hidden_t = low_hidden[:, cols].T
        found = nn(hidden_t, cotangent[...]).reshape(2, NY, DH, D)
        down[2 * j : 2 * j + 2] = found[:, :, 0:EARLY]
        big[1, 2 * j : 2 * j + 2, :, 16:24, :] = found[:, :, EARLY:DH]
        start(
            [
                send(
                    down.at[2 * j : 2 * j + 2, lax.rem(y + k, NY)],
                    down_y.at[k - 1, 2 * j : 2 * j + 2],
                    sem_dy,
                    peer_y(z, y, k),
                )
                for k in (2, 1, 3)
            ]
        )
        grad_second = grad_second + nt(grad_up_low[:, cols], w_up[:, cols])
    scaled = grad_second * gain_mlp[...]
    back = scale * (
        scaled
        - jnp.mean(scaled, axis=-1, keepdims=True)
        - hat * jnp.mean(scaled * hat, axis=-1, keepdims=True)
    )
    grad_resid = (cotangent[...].astype(F32) + back).astype(BF16)
    res_rows[...] = grad_resid
    grad_att = nt(grad_resid, w_out[...])
    att_grad[...] = grad_att.astype(BF16)
    att_t = grad_att.T.astype(BF16)
    for h in range(HEADS):
        mg_part[h] = nn(att_t[h * DH : (h + 1) * DH, :], wlow[h, 0:RB, :])
    mz_copies = [
        send(mg_part.at[lax.rem(z + k, NZ)], mg_z.at[k - 1], sem_mz, peer_z(z, y, k))
        for k in ORDER
    ]
    start(mz_copies)
    low_up_t[...] = low_up[...].astype(F32).T.astype(BF16)

    def grads_step(j, carry):
        cols = pl.ds(pl.multiple_of(j * D, D), D)
        up = nn(low_up_t[...], grad_up_low[:, cols])
        group = lax.div(j, 3)
        big[group, :, :, pl.ds(pl.multiple_of(8 * (j - 3 * group), 8), 8), :] = up.reshape(
            NZ, NY, 8, D
        )
        res_hold[...] += nn(low_hidden[:, cols], w_down[cols, :])
        return carry

    lax.fori_loop(0, FF // D, grads_step, 0)
    layer_out[...] = res_hold[...].astype(BF16)
    out = nn(att_rows[...].astype(F32).T.astype(BF16), res_rows[...])
    big[1, :, :, 8:16, :] = out.reshape(NZ, NY, 8, D)
    arrived(mg_z, sem_mz)
    total = mg_part[z]
    for k in range(NZ - 1):
        total = total + mg_z[k]
    mg_y[0] = total
    my_copies = [
        send(mg_y.at[0], mg_y.at[k], sem_my, peer_y(z, y, k)) for k in (2, 1, 3)
    ]
    start(my_copies)
    for group in range(2):
        start(
            [
                send(
                    big.at[group, :, lax.rem(y + k, NY)],
                    big_y.at[group, k - 1],
                    sem_by.at[group],
                    peer_y(z, y, k),
                )
                for k in (2, 1, 3)
            ]
        )

    def spread_big(group):
        arrived(big_y.at[group], sem_by.at[group])
        big_stage[group] = (
            (big[group, :, y] + big_y[group, 0]) + big_y[group, 1]
        ) + big_y[group, 2]
        start(
            [
                send(
                    big_stage.at[group, lax.rem(z + k, NZ)],
                    big_z.at[group, k - 1],
                    sem_bz.at[group],
                    peer_z(z, y, k),
                )
                for k in ORDER
            ]
        )

    arrived(down_y, sem_dy)
    down_stage[...] = ((down[:, y] + down_y[0]) + down_y[1]) + down_y[2]
    dz_copies = [
        send(down_stage.at[lax.rem(z + k, NZ)], down_z.at[k - 1], sem_dz, peer_z(z, y, k))
        for k in ORDER
    ]
    start(dz_copies)
    arrived(mg_y.at[1:NY], sem_my)
    grad = mg_y[y]
    for other in range(1, NY):
        grad = grad + mg_y[lax.rem(y + NY - other, NY)]
    mg_sum[...] = grad
    value_side = wide(nn, w_value[...], grad)
    d_attn = wide_tn(both, value_side)
    inner = jnp.sum(attention * d_attn, axis=0, keepdims=True)
    d_score = attention * (d_attn - inner)
    d_scores[...] = d_score
    d_both = wide(nt, query, d_score) + wide(nt, value_side, attention)
    d_field = (d_both[:, 0:M] + wide(nn, key_side, d_score)) / den
    d_geo = d_both[:, M : 2 * M] / geo_den
    den_grad = -jnp.sum(d_field * both[:, 0:M], axis=0, keepdims=True)
    geo_den_grad = -jnp.sum(d_geo * both[:, M : 2 * M], axis=0, keepdims=True)
    gbuf[z, 0:DH, :] = d_field
    gbuf[z, DH:CUT, :] = jnp.where(pick == 0, den_grad, jnp.where(pick == 1, geo_den_grad, 0.0))
    gbuf[z, CUT:SUMS, :] = d_geo

    def relay(step, way, half, origin):
        piece = gbuf.at[origin, half * CUT : CUT + half * DH]
        return pltpu.make_async_remote_copy(
            src_ref=piece,
            dst_ref=piece,
            send_sem=sem_g.at[0, way, half, step],
            recv_sem=sem_g.at[1, way, half, step],
            device_id=peer_z(z, y, 1 if way == 0 else NZ - 1),
            device_id_type=pl.DeviceIdType.MESH,
        )

    for half in range(2):
        for way in range(2):
            relay(0, way, half, z).start()
    def back_step(k, carry):
        step = lax.div(k + 1, 2)
        from_left = lax.rem(k, 2)
        h = lax.rem(z + NZ + (1 - 2 * from_left) * step, NZ)
        left = lax.rem(z + NZ - step, NZ)
        right = lax.rem(z + step, NZ)

        @pl.when(jnp.logical_and(from_left == 1, k < NZ - 3))
        def _():
            for half in range(2):
                relay(step - 1, 0, half, left).wait_recv()
                relay(step, 0, half, left).start()
                relay(step - 1, 1, half, right).wait_recv()
                relay(step, 1, half, right).start()

        @pl.when(k == NZ - 3)
        def _():
            relay(2, 0, 0, left).wait_recv()
            relay(3, 0, 0, left).start()
            relay(2, 1, 1, right).wait_recv()
            relay(3, 1, 1, right).start()
            relay(2, 0, 1, left).wait_recv()
            relay(2, 1, 0, right).wait_recv()

        @pl.when(k == NZ - 2)
        def _():
            spread_big(0)

        @pl.when(k == NZ - 1)
        def _():
            relay(3, 0, 0, left).wait_recv()
            relay(3, 1, 1, left).wait_recv()

        row = pl.multiple_of(h * DH, DH)
        spot = pl.multiple_of(lax.rem(h - z + NZ + 2, NZ) * DH, DH)
        num_m[h, pl.ds(row, DH), :] = gbuf[h, 0:DH, :].astype(BF16)
        geo_m[h, pl.ds(row, DH), :] = gbuf[h, CUT:SUMS, :].astype(BF16)
        factor = sharp[h]
        field_token = gbuf[h, 0:DH, :].astype(BF16)
        geo_token = gbuf[h, CUT:SUMS, :].astype(BF16)
        for b in range(3):
            rows = slice(b * RB, (b + 1) * RB)
            token = num_m[h] if b == 0 else geo_m[h]
            grad_w = nn(feats[rows, :], token)
            if b == 0:
                grad_w = grad_w + nn(att_grad[...], mixm[h])
                grad_w = (grad_w + gbuf[h, DH : DH + 1, :]) * valid
            else:
                grad_w = grad_w + gbuf[h, DH + 1 : DH + 2, :]
            share = shares[h, rows, :]
            inside = jnp.sum(share * grad_w, axis=-1, keepdims=True)
            low = (share * (grad_w - inside) * factor).astype(BF16)
            slice_part[...] += nn(mid_t[pl.ds(row, DH), rows], low).reshape(NY, 8, M)
            acc_mid[pl.ds(spot, DH), rows] = nt(w_slice[...], low).astype(BF16)
            acc_feat[pl.ds(spot, DH), rows] = nt(
                field_token if b == 0 else geo_token, wlow[h, rows, :]
            ).astype(BF16)
        return carry

    def narrow(which, rows):
        feat_half = nt(normed_t[...], acc_feat[rows, :])
        small[which, :, :, 0:8, :] = feat_half.reshape(NZ, NY, 8, D // 2)
        mid_half = nt(normed_t[...], acc_mid[rows, :])
        small[which, :, :, 8:SMALL, :] = mid_half.reshape(NZ, NY, 8, D // 2)
        start(
            [
                send(
                    small.at[which, :, lax.rem(y + k, NY)],
                    small_y.at[which, k - 1],
                    sem_sa if which == 0 else sem_sb,
                    peer_y(z, y, k),
                )
                for k in (2, 1, 3)
            ]
        )

    lax.fori_loop(0, HEADS // 2, back_step, 0)
    narrow(0, slice(0, D // 2))
    lax.fori_loop(HEADS // 2, HEADS, back_step, 0)
    start(
        [
            send(slice_part.at[lax.rem(y + k, NY)], slice_y.at[k - 1], sem_ly, peer_y(z, y, k))
            for k in (2, 1, 3)
        ]
    )
    narrow(1, slice(D // 2, D))
    both = both_in[...]
    back_rows = wide(nn, both, d_scores[...])
    cross = wide(nt, both[:, 0:M], back_rows)
    mix_part[:, 0:DH] = nn(cross, w_key[...], HIGH) * (1.0 / math.sqrt(DH))
    mix_part[:, DH : 2 * DH] = tn(cross, w_query[...], HIGH) * (1.0 / math.sqrt(DH))
    mix_part[:, 2 * DH : 3 * DH] = wide(nt, wide(nn, both, attn[...]), mg_sum[...])
    mix_part[:, 3 * DH : 4 * DH] = jnp.zeros((DH, DH), F32)
    arrived(slice_y, sem_ly)
    slice_z[0, 0:8, :] = ((slice_part[y] + slice_y[0]) + slice_y[1]) + slice_y[2]
    quarter = mix_part[pl.ds(pl.multiple_of(8 * y, 8), 8), :]
    slice_z[0, 8:16, 0 : 4 * DH] = quarter
    slice_z[0, 8:16, 4 * DH : M] = jnp.zeros((8, M - 4 * DH), F32)
    lz_copies = [send(slice_z.at[0], slice_z.at[k], sem_lz, peer_z(z, y, k)) for k in ORDER]
    start(lz_copies)
    spread_big(1)
    halves = []
    for which in range(2):
        arrived(small_y.at[which], sem_sa if which == 0 else sem_sb)
        halves.append(
            ((small[which, :, y] + small_y[which, 0]) + small_y[which, 1]) + small_y[which, 2]
        )
    turned = jnp.concatenate(halves, axis=2).reshape(NZ * SMALL, D)
    turned = pltpu.roll(turned, lax.rem(z + NZ - 2, NZ) * DH, 1)
    small_stage[...] = turned.reshape(NZ, SMALL, D)
    sz_copies = [
        send(small_stage.at[lax.rem(z + k, NZ)], small_z.at[k - 1], sem_sz, peer_z(z, y, k))
        for k in ORDER
    ]
    start(sz_copies)
    arrived(down_z, sem_dz)
    total = down_stage[z]
    for k in range(NZ - 1):
        total = total + down_z[k]
    packed[0:EARLY] = total
    arrived(slice_z.at[1:NZ], sem_lz)
    slices = slice_z[z]
    for other in range(1, NZ):
        slices = slices + slice_z[lax.rem(z + NZ - other, NZ)]
    slice_all[y] = slices
    la_copies = [
        send(slice_all.at[y], slice_all.at[y], sem_la, peer_y(z, y, k)) for k in (2, 1, 3)
    ]
    start(la_copies)
    for group in range(2):
        arrived(big_z.at[group], sem_bz.at[group])
        total = big_stage[group, z]
        for k in range(NZ - 1):
            total = total + big_z[group, k]
        if group == 0:
            packed[DH : DH + 24] = total
        else:
            packed[DH + 24 : DH + 40] = total[0:16]
            packed[EARLY:DH] = total[16:24]
    arrived(slice_all.at[1:NY], sem_la)
    packed[2 * DH + 24 : ROWS] = slice_all[:, 0:8, :].reshape(DH, M)
    mix = slice_all[:, 8:16, 0 : 4 * DH].reshape(DH, 4 * DH)
    for i in range(3):
        mix_grad[i] = mix[:, i * DH : (i + 1) * DH]
    arrived(small_z, sem_sz)
    total = small_stage[z]
    for k in range(NZ - 1):
        total = total + small_z[k]
    packed[2 * DH + 8 : 2 * DH + 24] = total
    for everything, sems in (
        (zbuf_f, sem_zf),
        (zbuf_g, sem_zg),
        (ybuf_f.at[1:NY], sem_yf),
        (ybuf_g.at[1:NY], sem_yg),
        (mbuf.at[1:NZ], sem_m),
        (mg_z, sem_mz),
        (mg_y.at[1:NY], sem_my),
        (down_y, sem_dy),
        (down_z, sem_dz),
        (big_y.at[0], sem_by.at[0]),
        (big_y.at[1], sem_by.at[1]),
        (big_z.at[0], sem_bz.at[0]),
        (big_z.at[1], sem_bz.at[1]),
        (small_y.at[0], sem_sa),
        (small_y.at[1], sem_sb),
        (small_z, sem_sz),
        (slice_y, sem_ly),
        (slice_z.at[1:NZ], sem_lz),
        (slice_all.at[1:NY], sem_la),
    ):
        sent(everything, sems)
    for step in range(4):
        for way in range(2):
            for half in range(2):
                if step < 3 or way == half:
                    relay(step, way, half, z).wait_send()


def result_kernel(
    layer_in,
    packed,
    mix_in,
    layer_out,
    feat_grad,
    mid_grad,
    out_grad,
    up_grad,
    down_grad,
    slice_grad,
    mix_grad,
):
    layer_out[...] = layer_in[...]
    down_grad[...] = packed[0:DH]
    for j in range(FF // D):
        up_grad[:, j * D : (j + 1) * D] = packed[DH + 8 * j : DH + 8 * j + 8]
    out_grad[...] = packed[2 * DH : 2 * DH + 8]
    feat_grad[...] = packed[2 * DH + 8 : 2 * DH + 16]
    mid_grad[...] = packed[2 * DH + 16 : 2 * DH + 24]
    slice_grad[...] = packed[2 * DH + 24 : ROWS]
    mix_grad[...] = mix_in[...]


def shape(dims, kind=F32):
    return jax.ShapeDtypeStruct(dims, kind)


def on_device(
    points,
    geometry,
    counts,
    cotangent,
    gain_attn,
    w_feat,
    w_mid,
    w_slice,
    sharpness,
    w_query,
    w_key,
    w_value,
    w_out,
    gain_mlp,
    w_up,
    w_down,
):
    vmem = pl.BlockSpec(memory_space=pltpu.VMEM)
    smem = pl.BlockSpec(memory_space=pltpu.SMEM)
    rows = 3 * RB

    def held(*dims):
        return pltpu.VMEM(dims, F32)

    def low(*dims):
        return pltpu.VMEM(dims, BF16)

    layer, packed, mix = pl.pallas_call(
        layer_kernel,
        out_shape=(shape((RB, D), BF16), shape((ROWS, D)), shape((3, DH, DH))),
        in_specs=[vmem] * 3 + [smem] * 2 + [vmem] * 11,
        out_specs=(vmem,) * 3,
        scratch_shapes=[
            low(D, rows),
            low(rows, D),
            low(D, rows),
            low(rows, D),
            low(D, rows),
            held(HEADS, rows, M),
            low(HEADS, rows, M),
            low(HEADS, D, M),
            low(HEADS, D, M),
            low(HEADS, D, M),
            low(HEADS, D, M),
            held(RB, FF),
            low(RB, FF),
            low(RB, D),
            low(D, RB),
            low(RB, FF),
            low(RB, D),
            low(RB, D),
            low(RB, D),
            held(RB, D),
            low(D, rows),
            low(D, rows),
            held(DH, 2 * M),
            held(2 * M, M),
            held(2 * M, M),
            held(DH, M),
            held(HEADS, DH, M),
            held(HEADS, CUT, M),
            held(NZ - 1, DH, M),
            held(NZ - 1, CUT, M),
            held(NY, DH, M),
            held(NY, CUT, M),
            held(HEADS, DH, M),
            held(HEADS, DH, M),
            held(NZ - 1, DH, M),
            held(NY, DH, M),
            held(HEADS, SUMS, M),
            held(DH, 4 * DH),
            held(NZ, NY, EARLY, D),
            held(NY - 1, NZ, EARLY, D),
            held(NZ, EARLY, D),
            held(NZ - 1, EARLY, D),
            held(2, NZ, NY, BIG, D),
            held(2, NY - 1, NZ, BIG, D),
            held(2, NZ, BIG, D),
            held(2, NZ - 1, BIG, D),
            held(2, NZ, NY, SMALL, D // 2),
            held(2, NY - 1, NZ, SMALL, D // 2),
            held(NZ, SMALL, D),
            held(NZ - 1, SMALL, D),
            held(NY, 8, M),
            held(NY - 1, 8, M),
            held(NZ, 16, M),
            held(NY, 16, M),
            pltpu.SemaphoreType.DMA((2, 2, 2, 4)),
        ]
        + [pltpu.SemaphoreType.DMA((2, 2))] * 2
        + [pltpu.SemaphoreType.DMA((2,))] * 15,
        compiler_params=pltpu.CompilerParams(
            collective_id=0, has_side_effects=True, vmem_limit_bytes=VMEM_BYTES
        ),
        name="layer",
    )(
        points,
        geometry,
        cotangent,
        counts,
        sharpness,
        gain_attn.reshape(1, D),
        gain_mlp.reshape(1, D),
        w_feat,
        w_mid,
        w_slice,
        w_query,
        w_key,
        w_value,
        w_out,
        w_up,
        w_down,
    )
    return pl.pallas_call(
        result_kernel,
        out_shape=(
            shape((RB, D), BF16),
            shape((8, D)),
            shape((8, D)),
            shape((8, D)),
            shape((8, FF)),
            shape((DH, D)),
            shape((DH, M)),
            shape((3, DH, DH)),
        ),
        in_specs=[vmem] * 3,
        out_specs=(vmem,) * 8,
        name="results",
    )(layer, packed, mix)


def solution(mesh):
    rows = P(("design", "pts"), None)
    return jax.shard_map(
        on_device,
        mesh=mesh,
        in_specs=(rows, rows, P(("design", "pts")), rows) + (P(),) * 12,
        out_specs=(rows,) * 6 + (P("design", None), P("design", None, None)),
        check_vma=False,
    )
```
